768 devices in a mesh: ctx: 24 (over z, core), tp: 32 (over x, y).
Axes of the slice: x: 4, y: 8, z: 12, core: 2. Of those that a mesh axis runs over, the one named last changes fastest.
Arguments:
- queries: bfloat16 [12288, 4096], P('ctx', 'tp'), may hold values from -15 to 15
- keys: bfloat16 [12288, 4096], P('ctx', 'tp'), may hold values from -15 to 15, as said below
- values: bfloat16 [12288, 4096], P('ctx', 'tp'), may hold values from -6 to 6, as said below
- doc_blocks: int32 [96], replicated, may hold values from 0 to 5, never falling along the last dimension, each value on 1 to 48 neighbouring positions
Outputs:
- attended: bfloat16 [12288, 4096], P('ctx', 'tp')
The draws below stay inside these ranges and needn't reach their ends.
Inputs may be any that keep to these rules, and one draw needn't show every extreme that they name: `doc_blocks`: ids never fall along the row; each document covers 1 to 48 blocks and one covers exactly that many. `keys`: copies of the same key-value head are equal. `values`: copies of the same key-value head are equal.
All inputs are finite; a program needn't handle non-finite values.
Results may differ from the reference program's by a relative error of at most 0.0047.
Values may be sent and summed in bfloat16 or wider, within the bound.
A program may use at most 32 MiB of HBM per device.

```python
import math
import jax
import jax.numpy as jnp
import numpy as np
from jax import lax

HQ = 32
KVH = 8
HD = 128
BLK = 128
COUNT = 6
CH = 256
L = 12288
S = 96
COPIES = 32
N_CTX = 24


def replicate_heads(array):
    spread = COPIES // KVH
    grouped = array.reshape(L, KVH, 1, HD)
    return jnp.broadcast_to(grouped, (L, KVH, spread, HD)).reshape(L, COPIES * HD)


def drawn_pair(key):
    base = jax.random.fold_in(key, 11)
    first_key, second_key = jax.random.split(base, 2)
    query_part = jnp.clip(jax.random.normal(first_key, (L, HQ * HD), jnp.float32), -4.0, 4.0)
    key_part = jnp.clip(jax.random.normal(second_key, (L, KVH * HD), jnp.float32), -4.0, 4.0)
    return (query_part, key_part)


def draw_queries(key, part):
    return drawn_pair(key)[0].astype(jnp.bfloat16)


def draw_keys(key, part):
    return replicate_heads(drawn_pair(key)[1]).astype(jnp.bfloat16)


def draw_values(key, part):
    value_key = jax.random.fold_in(key, 23)
    drawn = jnp.clip(jax.random.normal(value_key, (L, KVH * HD), jnp.float32), -6.0, 6.0)
    return replicate_heads(drawn).astype(jnp.bfloat16)


def split_up(number_of, total, limit, slope):
    portions = [(1 << 20) // math.isqrt(grade ** slope) + 1 for grade in range(2, number_of + 1)]
    surplus, counts = total - limit - (number_of - 1), [1] * (number_of - 1)
    while surplus > 0:
        candidates = [i for i in range(number_of - 1) if counts[i] < limit]
        whole, budget = sum([portions[i] for i in candidates]), surplus
        for i in candidates:
            more = min(limit - counts[i], max(1, budget * portions[i] // whole), surplus)
            counts[i] = counts[i] + more
            surplus = surplus - more
    return np.array([limit] + counts)


def uneven_parts(rng, amount, total, reach, skew):
    if amount == 2:
        one = jax.random.randint(rng, (), max(1, total - reach), min(reach, total - 1) + 1)
        return jnp.stack([one, total - one])
    tallies = jnp.asarray(split_up(amount, total, reach, skew), jnp.int32)
    couples = (amount - 1) // 2
    source_of, receiver = tallies[1:1 + 2 * couples:2], tallies[2:2 + 2 * couples:2]
    margin = jnp.minimum(source_of - 1, reach - receiver)
    moved = jax.random.randint(jax.random.fold_in(rng, 1), (couples,), 0, 1 << 20) % (margin + 1)
    tallies = tallies.at[1:1 + 2 * couples:2].set(source_of - moved).at[2:2 + 2 * couples:2].set(receiver + moved)
    return tallies[jax.random.permutation(jax.random.fold_in(rng, 2), amount)]


def setup_inputs(seed: int = 0) -> dict:
    streams_of = jax.random.split(jax.random.key(seed), 5)
    return {
        "queries": draw_queries(jax.random.fold_in(streams_of[4], 71), 0),
        "keys": draw_keys(jax.random.fold_in(streams_of[4], 71), 0),
        "values": draw_values(jax.random.fold_in(streams_of[4], 71), 0),
        "doc_blocks": jnp.searchsorted(jnp.cumsum(uneven_parts(streams_of[3], COUNT, S, S // 2, 0)), jnp.arange(S), side="right").astype(jnp.int32),
    }


def reference(queries, keys, values, doc_blocks):
    total_spans = 2 * N_CTX
    order_table = np.array([j // 2 if j % 2 == 0 else total_spans - 1 - j // 2 for j in range(total_spans)])
    inverse_table = np.argsort(order_table)

    def to_row_order(array):
        return array.reshape(total_spans, CH, array.shape[1])[inverse_table].reshape(L, array.shape[1])

    repeat_count = HQ // COPIES
    query_rows = to_row_order(queries).reshape(L, COPIES, repeat_count, HD)
    key_rows = to_row_order(keys).astype(jnp.float32).reshape(L, COPIES, HD).transpose(1, 0, 2)
    value_rows = to_row_order(values).astype(jnp.float32).reshape(L, COPIES, HD).transpose(1, 0, 2)
    doc_rows = jnp.repeat(doc_blocks, BLK).astype(jnp.int32)
    key_pos = jnp.arange(L, dtype=jnp.int32)
    score_scale = HD ** -0.5

    def one_span(index):
        start = (index * CH).astype(jnp.int32)
        query_part = lax.dynamic_slice_in_dim(query_rows, start, CH, 0).astype(jnp.float32).transpose(1, 0, 2, 3)
        query_doc = lax.dynamic_slice_in_dim(doc_rows, start, CH, 0)
        query_pos = start + jnp.arange(CH, dtype=jnp.int32)
        allowed = (query_doc[:, None] == doc_rows[None, :]) & (key_pos[None, :] <= query_pos[:, None])

        def one_copy(item):
            query_copy, key_copy, value_copy = item
            scores = jnp.einsum("qrd,kd->rqk", query_copy, key_copy) * score_scale
            scores = jnp.where(allowed, scores, -1e30)
            peak_value = jnp.max(scores, axis=-1, keepdims=True)
            weight = jnp.where(allowed, jnp.exp(scores - peak_value), 0.0)
            total = jnp.sum(weight, axis=-1, keepdims=True)
            probs = (weight / total).astype(jnp.bfloat16)
            probs = lax.optimization_barrier(probs).astype(jnp.float32)
            return jnp.einsum("rqk,kd->qrd", probs, value_copy)

        mixed = lax.map(one_copy, (query_part, key_rows, value_rows))
        return mixed.transpose(1, 0, 2, 3).reshape(CH, HQ * HD).astype(jnp.bfloat16)

    outputs = lax.map(one_span, jnp.arange(total_spans, dtype=jnp.int32))
    return outputs[order_table].reshape(L, HQ * HD)
```

```python
import functools

import jax
import jax.numpy as jnp
from jax import lax
from jax.experimental import pallas as pl
from jax.experimental.pallas import tpu as pltpu
from jax.sharding import PartitionSpec as P

HD = 128
BLK = 128
SPAN = 256
SHARE = 80
RING = SPAN - SHARE
MESH = pl.DeviceIdType.MESH
LOG2E = 1.4426950408889634
SCALE = HD**-0.5 * LOG2E
NEG = -1e30


def kernel(
    chips,
    doc_ref, q_hbm, k_hbm, v_hbm, out_ref,
    q_ref, kv, acc, peak, total,
    load_sem, ring_send, ring_recv, side_send, side_recv,
    mate_send, mate_recv, mate_side_send, mate_side_recv,
):
    ctx, tp = lax.axis_index("ctx"), lax.axis_index("tp")
    z, core = ctx // 2, ctx % 2
    odd = tp % 2
    shards = 2 * chips
    up = (lax.rem(ctx + 2, shards), tp)
    down = (lax.rem(ctx + shards - 2, shards), tp)
    mate = (2 * z + 1 - core, tp)
    side = (ctx, tp + 1 - 2 * odd)
    other = 1 - core

    loads = []
    for kind in range(2):
        for part, hbm in enumerate((k_hbm, v_hbm)):
            loads.append(
                pltpu.make_async_copy(
                    hbm.at[pl.ds(kind * SPAN, SPAN)], kv.at[z, kind, part, core], load_sem.at[2 * kind + part]
                )
            )
    loads.append(pltpu.make_async_copy(q_hbm, q_ref, load_sem.at[4]))
    for copy in loads:
        copy.start()

    barrier = pltpu.get_barrier_semaphore()
    for neighbour in (up, down, mate, side):
        pl.semaphore_signal(barrier, inc=1, device_id=neighbour, device_id_type=MESH)
    pl.semaphore_wait(barrier, 4)

    ring_at = pl.multiple_of(odd * SHARE, 16)
    give_at = pl.multiple_of(odd * RING, 16)
    take_at = pl.multiple_of((1 - odd) * RING, 16)

    def remote(ref, sends, recvs, index, device):
        return pltpu.make_async_remote_copy(
            src_ref=ref,
            dst_ref=ref,
            send_sem=sends.at[index],
            recv_sem=recvs.at[index],
            device_id=device,
            device_id_type=MESH,
        )

    def ring_copy(s, kind, device):
        return remote(
            kv.at[s, kind, :, core, pl.ds(ring_at, RING)], ring_send, ring_recv, (s, kind), device
        )

    def ring_arrival(s, kind):
        return ring_copy(s, kind, up)

    def side_copy(s, kind):
        return remote(kv.at[s, kind, :, core, pl.ds(give_at, SHARE)], side_send, side_recv, (s, kind), side)

    def side_arrival(s, kind):
        return remote(kv.at[s, kind, :, core, pl.ds(take_at, SHARE)], side_send, side_recv, (s, kind), side)

    def mate_ring(s, kind, who):
        return remote(kv.at[s, kind, :, who, pl.ds(ring_at, RING)], mate_send, mate_recv, (s, kind), mate)

    def mate_side(s, kind, who):
        return remote(
            kv.at[s, kind, :, who, pl.ds(take_at, SHARE)], mate_side_send, mate_side_recv, (s, kind), mate
        )

    def mate_own(kind, who):
        return remote(kv.at[z, kind, :, who], mate_send, mate_recv, (z, kind), mate)

    def own_second(kind, device, sems):
        return remote(
            kv.at[z, kind, :, core, pl.ds(ring_at, RING)], sems, ring_recv, (z, kind), device
        )

    for kind in range(2):
        loads[2 * kind].wait()
        loads[2 * kind + 1].wait()
        own_second(kind, up, ring_send).start()
        own_second(kind, down, side_send).start()
        mate_own(kind, core).start()
    loads[4].wait()

    low_block = 2 * ctx
    high_block = 2 * (2 * shards - 1 - ctx)

    def first_block(s, kind, j):
        return 2 * (2 * s + j) if kind == 0 else 2 * (2 * shards - 1 - 2 * s - j)

    def own(row, q_block, kind):
        q = q_ref[pl.ds(row, BLK)]
        k = kv[z, kind, 0].reshape(2 * SPAN, HD)
        v = kv[z, kind, 1].reshape(2 * SPAN, HD)
        s = lax.dot_general(q, k, (((1,), (1,)), ((), ())), preferred_element_type=jnp.float32)
        inside = lax.broadcasted_iota(jnp.int32, (BLK, BLK), 1) <= lax.broadcasted_iota(jnp.int32, (BLK, BLK), 0)
        parts = []
        for j in range(2):
            for half in range(2):
                k_block = first_block(z, kind, j) + half
                at = (2 * j + half) * BLK
                same = doc_ref[k_block] == doc_ref[q_block]
                before = jnp.where(same & (k_block < q_block), 0.0, NEG)
                at_or_before = jnp.where(same & (k_block <= q_block), 0.0, NEG)
                parts.append(s[:, at : at + BLK] * SCALE + jnp.where(inside, at_or_before, before))
        most = functools.reduce(jnp.maximum, parts)
        top = jnp.broadcast_to(jnp.max(most, axis=1, keepdims=True), (BLK, HD))
        weights = [jnp.exp2(part - top) for part in parts]
        peak[pl.ds(row, BLK)] = top
        total[pl.ds(row, BLK)] = functools.reduce(jnp.add, weights)
        joined = jnp.concatenate([w.astype(jnp.bfloat16) for w in weights], axis=1)
        acc[pl.ds(row, BLK)] = jnp.dot(joined, v, preferred_element_type=jnp.float32)

    def unit(row, q_block, s_chip, kind):
        q = q_ref[pl.ds(row, BLK)]
        k = kv[s_chip, kind, 0].reshape(2 * SPAN, HD)
        v = kv[s_chip, kind, 1].reshape(2 * SPAN, HD)
        s = lax.dot_general(q, k, (((1,), (1,)), ((), ())), preferred_element_type=jnp.float32)
        parts = []
        for j in range(2):
            for half in range(2):
                k_block = first_block(s_chip, kind, j) + half
                at = (2 * j + half) * BLK
                bias = jnp.where(doc_ref[k_block] == doc_ref[q_block], 0.0, NEG)
                parts.append(s[:, at : at + BLK] * SCALE + bias)
        most = functools.reduce(jnp.maximum, parts)
        old = peak[pl.ds(row, BLK)]
        top = jnp.maximum(old, jnp.max(most, axis=1, keepdims=True))
        shrink = jnp.exp2(old - top)
        weights = [jnp.exp2(part - top) for part in parts]
        peak[pl.ds(row, BLK)] = top
        total[pl.ds(row, BLK)] = total[pl.ds(row, BLK)] * shrink + functools.reduce(jnp.add, weights)
        joined = jnp.concatenate([w.astype(jnp.bfloat16) for w in weights], axis=1)
        acc[pl.ds(row, BLK)] = acc[pl.ds(row, BLK)] * shrink + jnp.dot(
            joined, v, preferred_element_type=jnp.float32
        )

    def units(base, q_first, s_chip, kind):
        for half in range(2):
            unit(base + half * BLK, q_first + half, s_chip, kind)

    for kind in range(2):
        mate_own(kind, other).wait_recv()
    for half in range(2):
        own(half * BLK, low_block + half, 0)
        own(SPAN + half * BLK, high_block + half, 1)

    @pl.when(z + z >= chips - 1)
    def _():
        units(SPAN, high_block, z, 0)

    def source(way, h):
        return lax.rem(z + 2 * chips - h, chips) if way == 0 else lax.rem(z + h, chips)

    half_ring = chips // 2
    limit = {(0, 0): half_ring, (1, 0): half_ring - 1, (0, 1): half_ring - 1, (1, 1): half_ring}

    def step(h, carry):
        for kind in range(2):
            for way in range(2):

                @pl.when(h <= limit[way, kind])
                def _():
                    s = source(way, h)
                    ring_arrival(s, kind).wait_recv()

                    @pl.when(h < limit[way, kind])
                    def _():
                        ring_copy(s, kind, up if way == 0 else down).start()

                    side_copy(s, kind).start()
                    mate_ring(s, kind, core).start()

        for kind in range(2):
            for way in range(2):

                @pl.when((h >= 2) & (h - 1 <= limit[way, kind]))
                def _():
                    s = source(way, h - 1)
                    side_arrival(s, kind).wait_recv()
                    mate_side(s, kind, core).start()

        for kind in range(2):
            for way in range(2):

                @pl.when((h >= 3) & (h - 2 <= limit[way, kind]))
                def _():
                    s = source(way, h - 2)
                    mate_ring(s, kind, other).wait_recv()
                    mate_side(s, kind, other).wait_recv()
                    if kind == 0:

                        @pl.when(s < z)
                        def _():
                            units(0, low_block, s, 0)

                        @pl.when(s + z >= chips - 1)
                        def _():
                            units(SPAN, high_block, s, 0)
                    else:

                        @pl.when(s > z)
                        def _():
                            units(SPAN, high_block, s, 1)

        return carry

    lax.fori_loop(1, half_ring + 3, step, 0)

    for row in range(0, 2 * SPAN, BLK):
        rows = pl.ds(row, BLK)
        out_ref[rows] = (acc[rows] / jnp.sum(total[rows], axis=1, keepdims=True)).astype(out_ref.dtype)

    for kind in range(2):
        own_second(kind, up, ring_send).wait_send()
        own_second(kind, down, side_send).wait_send()
        mate_own(kind, core).wait_send()

    def drain(h, carry):
        for kind in range(2):
            for way in range(2):

                @pl.when(h <= limit[way, kind])
                def _():
                    s = source(way, h)

                    @pl.when(h < limit[way, kind])
                    def _():
                        ring_copy(s, kind, up).wait_send()

                    side_copy(s, kind).wait_send()
                    mate_ring(s, kind, core).wait_send()
                    mate_side(s, kind, core).wait_send()

        return carry

    lax.fori_loop(1, half_ring + 1, drain, 0)


def body(queries, keys, values, doc_blocks):
    rows = queries.shape[0]
    chips = lax.axis_size("ctx") // 2
    sems = pltpu.SemaphoreType.DMA((chips, 2))
    return pl.pallas_call(
        functools.partial(kernel, chips),
        out_shape=jax.ShapeDtypeStruct((rows, HD), jnp.bfloat16),
        in_specs=[pl.BlockSpec(memory_space=pltpu.SMEM)] + [pl.BlockSpec(memory_space=pl.ANY)] * 3,
        out_specs=pl.BlockSpec(memory_space=pltpu.VMEM),
        scratch_shapes=[
            pltpu.VMEM((rows, HD), jnp.bfloat16),
            pltpu.VMEM((chips, 2, 2, 2, SPAN, HD), jnp.bfloat16),
            pltpu.VMEM((rows, HD), jnp.float32),
            pltpu.VMEM((rows, HD), jnp.float32),
            pltpu.VMEM((rows, HD), jnp.float32),
            pltpu.SemaphoreType.DMA((5,)),
        ]
        + [sems] * 8,
        compiler_params=pltpu.CompilerParams(collective_id=0, has_side_effects=True),
    )(doc_blocks, queries, keys, values)


def solution(mesh):
    return jax.shard_map(
        body,
        mesh=mesh,
        in_specs=(P("ctx", "tp"), P("ctx", "tp"), P("ctx", "tp"), P()),
        out_specs=P("ctx", "tp"),
        check_vma=False,
    )
```

```python
import functools

import jax
import jax.numpy as jnp
from jax import lax
from jax.experimental import pallas as pl
from jax.experimental.pallas import tpu as pltpu
from jax.sharding import PartitionSpec as P

HD = 128
BLK = 128
SPAN = 256
LONGEST = 48
STARTS = 4
MESH = pl.DeviceIdType.MESH
LOG2E = 1.4426950408889634
SCALE = HD**-0.5 * LOG2E
NEG = -1e30
FLOOR = -1e29
NONE = 15

PLANS = [
    (
        [
            [-1, 0, 1, 2, 3, 7, 8, 10, 10, 11, 0, 1],
            [-1, -1, 3, 1, 3, 4, 4, 9, 9, 11, 11, 1],
            [-1, -1, -1, 2, 2, 6, 4, 6, 6, 10, 11, 3],
            [-1, -1, -1, -1, 3, 4, 4, 3, 7, 11, 11, 3],
            [-1, -1, -1, -1, -1, 6, 4, 5, 6, 7, 8, 10],
            [-1, -1, -1, -1, -1, -1, 5, 8, 6, 8, 8, 9],
            [-1, -1, -1, -1, -1, -1, -1, 6, 6, 8, 8, 9],
            [-1, -1, -1, -1, -1, -1, -1, -1, 7, 10, 8, 10],
            [-1, -1, -1, -1, -1, -1, -1, -1, -1, 8, 11, 9],
            [-1, -1, -1, -1, -1, -1, -1, -1, -1, -1, 9, 10],
            [-1, -1, -1, -1, -1, -1, -1, -1, -1, -1, -1, 10],
            [-1, -1, -1, -1, -1, -1, -1, -1, -1, -1, -1, -1],
        ],
        [
            [-1, -1, -1, -1, -1, -1, -1, -1, -1, -1, -1, -1],
            [1, -1, -1, -1, -1, -1, -1, -1, -1, -1, -1, -1],
            [2, 2, -1, -1, -1, -1, -1, -1, -1, -1, -1, -1],
            [2, 0, 3, -1, -1, -1, -1, -1, -1, -1, -1, -1],
            [1, 2, 4, 2, -1, -1, -1, -1, -1, -1, -1, -1],
            [2, 2, 3, 5, 2, -1, -1, -1, -1, -1, -1, -1],
            [2, 2, 5, 4, 5, 6, -1, -1, -1, -1, -1, -1],
            [5, 0, 5, 4, 5, 7, 7, -1, -1, -1, -1, -1],
            [8, 0, 1, 1, 0, 4, 8, 6, -1, -1, -1, -1],
            [8, 0, 5, 5, 5, 8, 5, 8, 9, -1, -1, -1],
            [10, 2, 0, 2, 6, 6, 10, 6, 9, 10, -1, -1],
            [11, 0, 1, 6, 6, 6, 8, 8, 11, 10, 11, -1],
        ],
        [
            [5, 3, 17, 21, 23, 19, 7, 15, 13, 9, 11],
            [5, 0, 9, 17, 23, 13, 19, 7, 11, 15, 21],
            [9, 7, 0, 13, 11, 15, 2, 21, 17, 19, 23],
            [4, 11, 2, 9, 13, 0, 19, 17, 15, 21, 23],
            [4, 6, 13, 2, 15, 21, 17, 19, 11, 0, 23],
            [13, 15, 8, 6, 19, 2, 21, 4, 0, 17, 23],
            [8, 10, 15, 17, 21, 4, 6, 23, 2, 0, 19],
            [12, 6, 19, 0, 17, 21, 23, 8, 4, 2, 10],
            [19, 12, 14, 23, 8, 0, 10, 21, 6, 2, 4],
            [16, 21, 12, 2, 23, 6, 10, 0, 14, 4, 8],
            [0, 18, 23, 12, 2, 14, 6, 4, 8, 16, 10],
            [2, 20, 6, 4, 0, 16, 18, 12, 14, 8, 10],
        ],
    ),
    (
        [
            [-1, 0, -1, -1, -1, -1, -1, -1, -1, -1, -1, -1],
            [-1, -1, 1, 1, 2, 4, 4, 8, 10, 10, 1, 10],
            [-1, -1, -1, 4, 2, 3, 5, 9, 9, 4, 9, 10],
            [-1, -1, -1, -1, 5, 3, 7, 5, 6, 7, 9, 10],
            [-1, -1, -1, -1, -1, 6, 4, 6, 7, 7, 9, 8],
            [-1, -1, -1, -1, -1, -1, 5, 5, 7, 10, 7, 10],
            [-1, -1, -1, -1, -1, -1, -1, 6, 9, 7, 8, 9],
            [-1, -1, -1, -1, -1, -1, -1, -1, 7, 10, 8, 10],
            [-1, -1, -1, -1, -1, -1, -1, -1, -1, 8, 8, 10],
            [-1, -1, -1, -1, -1, -1, -1, -1, -1, -1, 9, 10],
            [-1, -1, -1, -1, -1, -1, -1, -1, -1, -1, -1, 10],
            [-1, -1, -1, -1, -1, -1, -1, -1, -1, -1, 11, -1],
        ],
        [
            [-1, -1, -1, -1, -1, -1, -1, -1, -1, -1, -1, -1],
            [1, -1, -1, -1, -1, -1, -1, -1, -1, -1, -1, -1],
            [2, 2, -1, -1, -1, -1, -1, -1, -1, -1, -1, -1],
            [2, 3, 3, -1, -1, -1, -1, -1, -1, -1, -1, -1],
            [2, 2, 4, 2, -1, -1, -1, -1, -1, -1, -1, -1],
            [1, 3, 3, 5, 3, -1, -1, -1, -1, -1, -1, -1],
            [1, 6, 1, 1, 3, 6, -1, -1, -1, -1, -1, -1],
            [7, 0, 5, 2, 5, 7, 7, -1, -1, -1, -1, -1],
            [7, 8, 1, 1, 5, 6, 7, 8, -1, -1, -1, -1],
            [9, 0, 5, 5, 5, 8, 7, 8, 9, -1, -1, -1],
            [10, 0, 5, 5, 3, 10, 5, 8, 10, 10, -1, -1],
            [-1, -1, -1, -1, -1, -1, -1, -1, -1, -1, 11, -1],
        ],
        [
            [5, 3, 15, 7, 19, 13, 21, 9, 11, 17],
            [0, 5, 7, 13, 11, 17, 15, 9, 19, 21],
            [7, 2, 9, 11, 13, 15, 17, 21, 19],
            [11, 2, 4, 13, 21, 9, 17, 15, 19],
            [4, 6, 2, 11, 15, 19, 13, 17, 21],
            [6, 13, 15, 21, 19, 8, 4, 17, 2],
            [10, 8, 15, 17, 21, 6, 19, 2, 4],
            [17, 10, 12, 6, 19, 8, 21, 4, 2],
            [19, 14, 21, 10, 2, 4, 8, 6, 12],
            [21, 16, 4, 2, 12, 6, 14, 8, 10],
            [2, 23, 22, 16, 18, 14, 10, 4, 6, 8, 12],
            [20, 2, 16, 18, 14, 10, 12, 4, 8, 6],
        ],
    ),
    (
        [
            [-1, 2, 0, -1, -1, -1, -1, -1, -1, -1, -1, -1],
            [-1, -1, 1, -1, -1, -1, -1, -1, -1, -1, -1, -1],
            [-1, -1, -1, 2, 2, 3, 5, 10, 6, 10, 2, 10],
            [-1, -1, -1, -1, 3, 3, 9, 9, 9, 5, 9, 10],
            [-1, -1, -1, -1, -1, 4, 5, 5, 7, 6, 9, 9],
            [-1, -1, -1, -1, -1, -1, 5, 6, 9, 7, 9, 9],
            [-1, -1, -1, -1, -1, -1, -1, 6, 7, 7, 11, 9],
            [-1, -1, -1, -1, -1, -1, -1, -1, 9, 7, 9, 10],
            [-1, -1, -1, -1, -1, -1, -1, -1, -1, 8, 9, 10],
            [-1, -1, -1, -1, -1, -1, -1, -1, -1, -1, 11, 9],
            [-1, -1, -1, -1, -1, -1, -1, -1, -1, 10, -1, 10],
            [-1, -1, -1, -1, -1, -1, -1, -1, -1, 11, 11, -1],
        ],
        [
            [-1, -1, -1, -1, -1, -1, -1, -1, -1, -1, -1, -1],
            [1, -1, -1, -1, -1, -1, -1, -1, -1, -1, -1, -1],
            [2, 0, -1, -1, -1, -1, -1, -1, -1, -1, -1, -1],
            [1, 3, 1, -1, -1, -1, -1, -1, -1, -1, -1, -1],
            [2, 0, 4, 2, -1, -1, -1, -1, -1, -1, -1, -1],
            [4, 3, 3, 4, 5, -1, -1, -1, -1, -1, -1, -1],
            [2, 2, 6, 2, 2, 6, -1, -1, -1, -1, -1, -1],
            [1, 7, 3, 5, 5, 7, 5, -1, -1, -1, -1, -1],
            [1, 8, 1, 7, 5, 7, 7, 8, -1, -1, -1, -1],
            [9, 0, 0, 4, 9, 4, 5, 8, 9, -1, -1, -1],
            [-1, -1, -1, -1, -1, -1, -1, -1, -1, 10, -1, -1],
            [-1, -1, -1, -1, -1, -1, -1, -1, -1, 10, 11, -1],
        ],
        [
            [3, 5, 7, 9, 19, 11, 13, 15, 17],
            [7, 0, 15, 17, 5, 13, 9, 11, 19],
            [0, 2, 9, 7, 13, 17, 11, 15, 19],
            [4, 9, 11, 17, 13, 15, 19],
            [6, 11, 4, 19, 15, 13, 17],
            [6, 8, 13, 15, 4, 17, 19],
            [10, 8, 17, 15, 4, 19, 6],
            [12, 17, 10, 19, 8, 4, 6],
            [19, 12, 14, 8, 6, 4, 10],
            [21, 20, 14, 16, 12, 6, 22, 10, 4, 23, 8],
            [4, 23, 14, 22, 16, 18, 6, 10, 12, 8],
            [18, 20, 4, 12, 14, 16, 10, 6, 8],
        ],
    ),
    (
        [
            [-1, 0, 0, 2, -1, -1, -1, -1, -1, -1, -1, -1],
            [-1, -1, 1, 2, -1, -1, -1, -1, -1, -1, -1, -1],
            [-1, -1, -1, 2, -1, -1, -1, -1, -1, -1, -1, -1],
            [-1, -1, -1, -1, 5, 3, 5, 9, 9, 6, 9, 10],
            [-1, -1, -1, -1, -1, 6, 4, 8, 6, 8, 9, 7],
            [-1, -1, -1, -1, -1, -1, 5, 6, 7, 8, 11, 7],
            [-1, -1, -1, -1, -1, -1, -1, 8, 6, 8, 11, 9],
            [-1, -1, -1, -1, -1, -1, -1, -1, 9, 7, 11, 9],
            [-1, -1, -1, -1, -1, -1, -1, -1, -1, 8, 9, 10],
            [-1, -1, -1, -1, -1, -1, -1, -1, 10, -1, 9, 10],
            [-1, -1, -1, -1, -1, -1, -1, -1, 10, 11, -1, 10],
            [-1, -1, -1, -1, -1, -1, -1, -1, 10, 11, 11, -1],
        ],
        [
            [-1, -1, -1, -1, -1, -1, -1, -1, -1, -1, -1, -1],
            [1, -1, -1, -1, -1, -1, -1, -1, -1, -1, -1, -1],
            [2, 2, -1, -1, -1, -1, -1, -1, -1, -1, -1, -1],
            [3, 0, 0, -1, -1, -1, -1, -1, -1, -1, -1, -1],
            [2, 0, 4, 2, -1, -1, -1, -1, -1, -1, -1, -1],
            [2, 0, 5, 4, 2, -1, -1, -1, -1, -1, -1, -1],
            [2, 2, 6, 2, 2, 3, -1, -1, -1, -1, -1, -1],
            [7, 2, 7, 2, 5, 7, 7, -1, -1, -1, -1, -1],
            [8, 0, 5, 5, 5, 8, 5, 6, -1, -1, -1, -1],
            [-1, -1, -1, -1, -1, -1, -1, -1, 9, -1, -1, -1],
            [-1, -1, -1, -1, -1, -1, -1, -1, 10, 8, -1, -1],
            [-1, -1, -1, -1, -1, -1, -1, -1, 9, 10, 11, -1],
        ],
        [
            [3, 5, 7, 17, 9, 15, 11, 13],
            [0, 5, 7, 17, 13, 9, 15, 11],
            [0, 2, 9, 11, 13, 15, 7, 17],
            [4, 0, 2, 9, 13, 17, 15, 11],
            [6, 11, 17, 13, 15],
            [6, 17, 15, 8, 13],
            [8, 10, 6, 15, 17],
            [12, 10, 8, 17, 6],
            [19, 12, 21, 20, 8, 22, 14, 10, 23, 18, 6],
            [16, 22, 14, 23, 12, 21, 6, 8, 20, 10],
            [23, 22, 18, 16, 14, 6, 12, 8, 10],
            [20, 14, 18, 12, 16, 10, 8, 6],
        ],
    ),
    (
        [
            [-1, 0, 1, 1, 3, -1, -1, -1, -1, -1, -1, -1],
            [-1, -1, 1, 2, 2, -1, -1, -1, -1, -1, -1, -1],
            [-1, -1, -1, 2, 3, -1, -1, -1, -1, -1, -1, -1],
            [-1, -1, -1, -1, 3, -1, -1, -1, -1, -1, -1, -1],
            [-1, -1, -1, -1, -1, 6, 4, 8, 6, 10, 8, 10],
            [-1, -1, -1, -1, -1, -1, 5, 6, 6, 8, 7, 10],
            [-1, -1, -1, -1, -1, -1, -1, 6, 7, 10, 8, 10],
            [-1, -1, -1, -1, -1, -1, -1, -1, 9, 7, 9, 10],
            [-1, -1, -1, -1, -1, -1, -1, 8, -1, 11, 11, 8],
            [-1, -1, -1, -1, -1, -1, -1, 9, 9, -1, 11, 9],
            [-1, -1, -1, -1, -1, -1, -1, 9, 7, 10, -1, 10],
            [-1, -1, -1, -1, -1, -1, -1, 9, 9, 10, 11, -1],
        ],
        [
            [-1, -1, -1, -1, -1, -1, -1, -1, -1, -1, -1, -1],
            [1, -1, -1, -1, -1, -1, -1, -1, -1, -1, -1, -1],
            [2, 0, -1, -1, -1, -1, -1, -1, -1, -1, -1, -1],
            [3, 0, 3, -1, -1, -1, -1, -1, -1, -1, -1, -1],
            [4, 2, 4, 2, -1, -1, -1, -1, -1, -1, -1, -1],
            [4, 4, 4, 2, 5, -1, -1, -1, -1, -1, -1, -1],
            [1, 6, 1, 4, 5, 6, -1, -1, -1, -1, -1, -1],
            [7, 0, 4, 4, 7, 6, 7, -1, -1, -1, -1, -1],
            [-1, -1, -1, -1, -1, -1, -1, 8, -1, -1, -1, -1],
            [-1, -1, -1, -1, -1, -1, -1, 8, 9, -1, -1, -1],
            [-1, -1, -1, -1, -1, -1, -1, 8, 9, 10, -1, -1],
            [-1, -1, -1, -1, -1, -1, -1, 8, 9, 10, 11, -1],
        ],
        [
            [3, 5, 7, 9, 15, 11, 13],
            [0, 5, 7, 13, 11, 9, 15],
            [2, 0, 7, 9, 11, 13, 15],
            [0, 4, 2, 9, 15, 13, 11],
            [6, 11, 2, 15, 0, 4, 13],
            [13, 8, 15],
            [8, 10, 15],
            [12, 17, 16, 18, 19, 10, 20, 21, 8, 22, 23],
            [19, 18, 12, 21, 8, 14, 10, 23, 20, 22],
            [21, 20, 14, 23, 22, 16, 10, 12, 8],
            [23, 22, 14, 12, 8, 16, 10, 18],
            [16, 18, 20, 14, 12, 8, 10],
        ],
    ),
    (
        [
            [-1, 2, 0, 2, 2, 4, -1, -1, -1, -1, -1, -1],
            [-1, -1, 1, 2, 2, 3, -1, -1, -1, -1, -1, -1],
            [-1, -1, -1, 4, 2, 4, -1, -1, -1, -1, -1, -1],
            [-1, -1, -1, -1, 5, 3, -1, -1, -1, -1, -1, -1],
            [-1, -1, -1, -1, -1, 4, -1, -1, -1, -1, -1, -1],
            [-1, -1, -1, -1, -1, -1, 5, 8, 6, 7, 8, 10],
            [-1, -1, -1, -1, -1, -1, -1, 6, 7, 7, 8, 9],
            [-1, -1, -1, -1, -1, -1, 7, -1, 6, 8, 7, 10],
            [-1, -1, -1, -1, -1, -1, 7, 8, -1, 8, 8, 10],
            [-1, -1, -1, -1, -1, -1, 7, 9, 7, -1, 9, 10],
            [-1, -1, -1, -1, -1, -1, 7, 10, 7, 11, -1, 10],
            [-1, -1, -1, -1, -1, -1, 8, 8, 9, 11, 11, -1],
        ],
        [
            [-1, -1, -1, -1, -1, -1, -1, -1, -1, -1, -1, -1],
            [1, -1, -1, -1, -1, -1, -1, -1, -1, -1, -1, -1],
            [2, 0, -1, -1, -1, -1, -1, -1, -1, -1, -1, -1],
            [3, 0, 0, -1, -1, -1, -1, -1, -1, -1, -1, -1],
            [3, 3, 1, 4, -1, -1, -1, -1, -1, -1, -1, -1],
            [5, 0, 3, 5, 3, -1, -1, -1, -1, -1, -1, -1],
            [6, 4, 4, 4, 6, 6, -1, -1, -1, -1, -1, -1],
            [-1, -1, -1, -1, -1, -1, 7, -1, -1, -1, -1, -1],
            [-1, -1, -1, -1, -1, -1, 8, 6, -1, -1, -1, -1],
            [-1, -1, -1, -1, -1, -1, 7, 8, 9, -1, -1, -1],
            [-1, -1, -1, -1, -1, -1, 8, 8, 9, 10, -1, -1],
            [-1, -1, -1, -1, -1, -1, 7, 10, 10, 10, 11, -1],
        ],
        [
            [3, 5, 7, 11, 9, 13],
            [0, 5, 7, 9, 11, 13],
            [0, 2, 11, 7, 13, 9],
            [9, 0, 2, 11, 4, 13],
            [4, 0, 13, 2, 6, 11],
            [6, 8, 13, 4, 0, 2],
            [10, 15, 17, 14, 16, 18, 20, 21, 19, 23, 22],
            [12, 16, 18, 20, 19, 17, 23, 10, 21, 22],
            [19, 10, 21, 12, 23, 14, 22, 18, 20],
            [21, 22, 16, 12, 23, 20, 14, 10],
            [23, 22, 14, 16, 18, 10, 12],
            [20, 14, 16, 18, 12, 10],
        ],
    ),
    (
        [
            [-1, 0, 0, 1, 2, 4, 5, -1, -1, -1, -1, -1],
            [-1, -1, 1, 2, 3, 3, 4, -1, -1, -1, -1, -1],
            [-1, -1, -1, 2, 5, 3, 5, -1, -1, -1, -1, -1],
            [-1, -1, -1, -1, 5, 3, 5, -1, -1, -1, -1, -1],
            [-1, -1, -1, -1, -1, 4, 5, -1, -1, -1, -1, -1],
            [-1, -1, -1, -1, -1, -1, 5, -1, -1, -1, -1, -1],
            [-1, -1, -1, -1, -1, 6, -1, 6, 9, 6, 9, 9],
            [-1, -1, -1, -1, -1, 6, 7, -1, 7, 8, 9, 6],
            [-1, -1, -1, -1, -1, 7, 7, 9, -1, 8, 9, 9],
            [-1, -1, -1, -1, -1, 6, 10, 6, 10, -1, 9, 9],
            [-1, -1, -1, -1, -1, 7, 7, 8, 10, 11, -1, 10],
            [-1, -1, -1, -1, -1, 11, 5, 9, 9, 11, 11, -1],
        ],
        [
            [-1, -1, -1, -1, -1, -1, -1, -1, -1, -1, -1, -1],
            [1, -1, -1, -1, -1, -1, -1, -1, -1, -1, -1, -1],
            [1, 2, -1, -1, -1, -1, -1, -1, -1, -1, -1, -1],
            [3, 0, 3, -1, -1, -1, -1, -1, -1, -1, -1, -1],
            [4, 4, 1, 4, -1, -1, -1, -1, -1, -1, -1, -1],
            [4, 4, 4, 4, 5, -1, -1, -1, -1, -1, -1, -1],
            [-1, -1, -1, -1, -1, 6, -1, -1, -1, -1, -1, -1],
            [-1, -1, -1, -1, -1, 6, 7, -1, -1, -1, -1, -1],
            [-1, -1, -1, -1, -1, 6, 7, 8, -1, -1, -1, -1],
            [-1, -1, -1, -1, -1, 6, 9, 6, 7, -1, -1, -1],
            [-1, -1, -1, -1, -1, 6, 10, 6, 7, 6, -1, -1],
            [-1, -1, -1, -1, -1, 11, 5, 8, 10, 10, 11, -1],
        ],
        [
            [3, 7, 9, 5, 11],
            [0, 5, 9, 7, 11],
            [0, 2, 7, 11, 9],
            [4, 0, 2, 9, 11],
            [11, 0, 6, 4, 2],
            [6, 8, 13, 12, 4, 15, 14, 23, 19, 22, 21, 0, 17, 2, 16, 18, 20],
            [10, 15, 14, 19, 6, 21, 8, 17, 4, 18, 23, 16, 22, 2, 20, 0],
            [17, 12, 16, 19, 20, 21, 22, 18, 23],
            [14, 20, 18, 23, 22, 19, 12, 21],
            [16, 22, 12, 14, 23, 20, 21],
            [18, 23, 22, 16, 12, 14],
            [18, 20, 16, 14, 12],
        ],
    ),
    (
        [
            [-1, 0, 1, 2, 5, 2, 7, 5, -1, -1, -1, -1],
            [-1, -1, 3, 1, 3, 4, 5, 6, -1, -1, -1, -1],
            [-1, -1, -1, 4, 2, 4, 5, 6, -1, -1, -1, -1],
            [-1, -1, -1, -1, 3, 4, 5, 6, -1, -1, -1, -1],
            [-1, -1, -1, -1, -1, 4, 7, 5, -1, -1, -1, -1],
            [-1, -1, -1, -1, -1, -1, 5, 5, -1, -1, -1, -1],
            [-1, -1, -1, -1, -1, -1, -1, 6, -1, -1, -1, -1],
            [-1, -1, -1, -1, 6, 4, 7, -1, 9, 7, 9, 9],
            [-1, -1, -1, -1, 8, 4, 5, 8, -1, 7, 9, 7],
            [-1, -1, -1, -1, 10, 7, 7, 8, 9, -1, 9, 10],
            [-1, -1, -1, -1, 11, 6, 8, 9, 10, 11, -1, 10],
            [-1, -1, -1, -1, 11, 4, 8, 8, 11, 11, 11, -1],
        ],
        [
            [-1, -1, -1, -1, -1, -1, -1, -1, -1, -1, -1, -1],
            [1, -1, -1, -1, -1, -1, -1, -1, -1, -1, -1, -1],
            [1, 2, -1, -1, -1, -1, -1, -1, -1, -1, -1, -1],
            [2, 2, 3, -1, -1, -1, -1, -1, -1, -1, -1, -1],
            [4, 3, 3, 4, -1, -1, -1, -1, -1, -1, -1, -1],
            [-1, -1, -1, -1, 5, -1, -1, -1, -1, -1, -1, -1],
            [-1, -1, -1, -1, 6, 6, -1, -1, -1, -1, -1, -1],
            [-1, -1, -1, -1, 6, 4, 7, -1, -1, -1, -1, -1],
            [-1, -1, -1, -1, 6, 6, 8, 6, -1, -1, -1, -1],
            [-1, -1, -1, -1, 6, 6, 8, 6, 9, -1, -1, -1],
            [-1, -1, -1, -1, 10, 4, 5, 8, 9, 10, -1, -1],
            [-1, -1, -1, -1, 11, 4, 5, 8, 10, 10, 11, -1],
        ],
        [
            [3, 9, 7, 5],
            [0, 5, 7, 9],
            [0, 7, 2, 9],
            [2, 9, 0, 4],
            [6, 4, 11, 2, 13, 16, 21, 17, 23, 0, 22, 15, 18, 14, 20, 19],
            [8, 13, 0, 6, 4, 2, 17, 16, 21, 23, 19, 22, 18, 15, 20, 14],
            [10, 17, 15, 14, 19, 6, 20, 4, 8, 2, 22, 16, 18, 21, 0, 23],
            [10, 16, 12, 8, 17, 18, 0, 19, 22, 21, 6, 23, 4, 20, 2],
            [19, 18, 20, 22, 21, 23, 14],
            [21, 14, 22, 23, 16, 20],
            [18, 23, 22, 14, 16],
            [20, 18, 14, 16],
        ],
    ),
    (
        [
            [-1, 2, 0, 2, 3, 2, 5, 6, 6, -1, -1, -1],
            [-1, -1, 3, 1, 3, 3, 5, 6, 6, -1, -1, -1],
            [-1, -1, -1, 4, 5, 2, 7, 5, 7, -1, -1, -1],
            [-1, -1, -1, -1, 5, 3, 5, 8, 6, -1, -1, -1],
            [-1, -1, -1, -1, -1, 4, 5, 8, 6, -1, -1, -1],
            [-1, -1, -1, -1, -1, -1, 5, 6, 7, -1, -1, -1],
            [-1, -1, -1, -1, -1, -1, -1, 6, 6, -1, -1, -1],
            [-1, -1, -1, -1, -1, -1, -1, -1, 7, -1, -1, -1],
            [-1, -1, -1, 9, 3, 6, 7, 9, -1, 8, 9, 10],
            [-1, -1, -1, 10, 5, 7, 5, 9, 7, -1, 9, 9],
            [-1, -1, -1, 9, 5, 7, 5, 10, 9, 10, -1, 10],
            [-1, -1, -1, 4, 11, 4, 7, 9, 9, 11, 11, -1],
        ],
        [
            [-1, -1, -1, -1, -1, -1, -1, -1, -1, -1, -1, -1],
            [1, -1, -1, -1, -1, -1, -1, -1, -1, -1, -1, -1],
            [1, 2, -1, -1, -1, -1, -1, -1, -1, -1, -1, -1],
            [1, 3, 3, -1, -1, -1, -1, -1, -1, -1, -1, -1],
            [-1, -1, -1, 4, -1, -1, -1, -1, -1, -1, -1, -1],
            [-1, -1, -1, 4, 5, -1, -1, -1, -1, -1, -1, -1],
            [-1, -1, -1, 4, 6, 6, -1, -1, -1, -1, -1, -1],
            [-1, -1, -1, 5, 3, 7, 7, -1, -1, -1, -1, -1],
            [-1, -1, -1, 5, 5, 7, 5, 8, -1, -1, -1, -1],
            [-1, -1, -1, 5, 5, 7, 5, 9, 7, -1, -1, -1],
            [-1, -1, -1, 9, 3, 7, 7, 9, 7, 10, -1, -1],
            [-1, -1, -1, 11, 3, 3, 5, 9, 9, 10, 11, -1],
        ],
        [
            [3, 5, 7],
            [5, 7, 0],
            [0, 7, 2],
            [2, 9, 0, 11, 23, 13, 15, 4, 16, 18, 17, 22, 21, 19, 20],
            [11, 13, 2, 4, 6, 22, 0, 23, 17, 15, 19, 16, 18, 20, 21],
            [4, 13, 6, 15, 8, 0, 17, 2, 19, 18, 20, 23, 22, 21, 16],
            [10, 15, 6, 8, 0, 17, 4, 2, 16, 19, 18, 21, 20, 22, 23],
            [12, 17, 19, 18, 10, 20, 4, 16, 21, 22, 0, 23, 6, 2, 8],
            [12, 14, 19, 18, 20, 10, 4, 22, 6, 8, 23, 21, 0, 2],
            [16, 21, 20, 22, 23],
            [18, 23, 22, 16],
            [18, 20, 16],
        ],
    ),
    (
        [
            [-1, 2, 0, 2, 3, 4, 5, 8, 3, 8, -1, -1],
            [-1, -1, 3, 1, 5, 6, 3, 8, 6, 8, -1, -1],
            [-1, -1, -1, 2, 3, 4, 7, 5, 7, 7, -1, -1],
            [-1, -1, -1, -1, 3, 4, 7, 5, 7, 8, -1, -1],
            [-1, -1, -1, -1, -1, 4, 7, 5, 7, 7, -1, -1],
            [-1, -1, -1, -1, -1, -1, 5, 5, 9, 7, -1, -1],
            [-1, -1, -1, -1, -1, -1, -1, 8, 6, 8, -1, -1],
            [-1, -1, -1, -1, -1, -1, -1, -1, 9, 7, -1, -1],
            [-1, -1, -1, -1, -1, -1, -1, -1, -1, 8, -1, -1],
            [-1, -1, 10, 2, 5, 6, 9, 5, 10, -1, 9, 10],
            [-1, -1, 10, 4, 2, 4, 8, 6, 10, 8, -1, 10],
            [-1, -1, 10, 11, 3, 6, 10, 8, 10, 8, 11, -1],
        ],
        [
            [-1, -1, -1, -1, -1, -1, -1, -1, -1, -1, -1, -1],
            [1, -1, -1, -1, -1, -1, -1, -1, -1, -1, -1, -1],
            [2, 2, -1, -1, -1, -1, -1, -1, -1, -1, -1, -1],
            [-1, -1, 3, -1, -1, -1, -1, -1, -1, -1, -1, -1],
            [-1, -1, 4, 4, -1, -1, -1, -1, -1, -1, -1, -1],
            [-1, -1, 3, 5, 5, -1, -1, -1, -1, -1, -1, -1],
            [-1, -1, 4, 2, 6, 6, -1, -1, -1, -1, -1, -1],
            [-1, -1, 3, 6, 3, 4, 7, -1, -1, -1, -1, -1],
            [-1, -1, 4, 4, 6, 4, 8, 5, -1, -1, -1, -1],
            [-1, -1, 3, 6, 5, 6, 9, 6, 7, -1, -1, -1],
            [-1, -1, 9, 2, 2, 6, 8, 8, 9, 10, -1, -1],
            [-1, -1, 11, 2, 3, 3, 7, 8, 11, 10, 11, -1],
        ],
        [
            [3, 5],
            [5, 0],
            [0, 9, 7, 2, 20, 11, 23, 18, 13, 21, 15, 17, 22, 19],
            [2, 4, 0, 9, 11, 15, 22, 19, 23, 18, 17, 13, 20, 21],
            [6, 11, 4, 13, 0, 17, 20, 15, 22, 19, 2, 23, 18, 21],
            [8, 13, 6, 4, 19, 0, 2, 18, 17, 20, 23, 22, 15, 21],
            [10, 15, 17, 19, 2, 18, 20, 8, 22, 0, 21, 23, 6, 4],
            [10, 8, 19, 12, 23, 6, 4, 21, 20, 0, 18, 2, 17, 22],
            [20, 12, 23, 18, 21, 0, 2, 22, 8, 14, 19, 10, 6, 4],
            [21, 14, 16, 23, 10, 20, 12, 8, 0, 2, 22, 4, 6],
            [18, 23, 22],
            [20, 18],
        ],
    ),
    (
        [
            [-1, 2, 0, 0, 3, 4, 2, 6, 9, 1, 9, -1],
            [-1, -1, 1, 2, 3, 2, 5, 6, 10, 10, 2, -1],
            [-1, -1, -1, 4, 5, 2, 5, 8, 6, 8, 8, -1],
            [-1, -1, -1, -1, 3, 7, 4, 6, 7, 6, 9, -1],
            [-1, -1, -1, -1, -1, 7, 5, 4, 7, 8, 9, -1],
            [-1, -1, -1, -1, -1, -1, 7, 5, 6, 7, 9, -1],
            [-1, -1, -1, -1, -1, -1, -1, 6, 7, 7, 9, -1],
            [-1, -1, -1, -1, -1, -1, -1, -1, 7, 7, 9, -1],
            [-1, -1, -1, -1, -1, -1, -1, -1, -1, 8, 9, -1],
            [-1, -1, -1, -1, -1, -1, -1, -1, -1, -1, 9, -1],
            [-1, 10, 1, 2, 5, 7, 5, 10, 10, 10, -1, 1],
            [-1, 9, 11, 2, 5, 9, 9, 6, 9, 11, 11, -1],
        ],
        [
            [-1, -1, -1, -1, -1, -1, -1, -1, -1, -1, -1, -1],
            [1, -1, -1, -1, -1, -1, -1, -1, -1, -1, -1, -1],
            [-1, 2, -1, -1, -1, -1, -1, -1, -1, -1, -1, -1],
            [-1, 2, 3, -1, -1, -1, -1, -1, -1, -1, -1, -1],
            [-1, 2, 3, 4, -1, -1, -1, -1, -1, -1, -1, -1],
            [-1, 3, 1, 5, 3, -1, -1, -1, -1, -1, -1, -1],
            [-1, 3, 3, 6, 3, 6, -1, -1, -1, -1, -1, -1],
            [-1, 4, 4, 5, 6, 6, 7, -1, -1, -1, -1, -1],
            [-1, 2, 4, 2, 8, 4, 5, 8, -1, -1, -1, -1],
            [-1, 8, 1, 7, 5, 7, 5, 8, 9, -1, -1, -1],
            [-1, 2, 10, 2, 2, 3, 4, 8, 10, 8, -1, -1],
            [-1, 11, 11, 2, 3, 3, 7, 8, 10, 8, 11, -1],
        ],
        [
            [3],
            [5, 0, 7, 20, 23, 11, 13, 9, 19, 21, 15, 17, 22],
            [0, 7, 2, 9, 21, 13, 23, 17, 22, 20, 11, 15, 19],
            [0, 9, 11, 13, 2, 21, 23, 19, 17, 15, 22, 4, 20],
            [6, 17, 0, 15, 4, 11, 13, 21, 2, 20, 23, 19, 22],
            [13, 4, 15, 8, 2, 17, 20, 0, 19, 22, 21, 6, 23],
            [15, 0, 6, 4, 10, 8, 2, 17, 22, 20, 21, 19, 23],
            [8, 17, 10, 12, 20, 19, 21, 0, 6, 23, 2, 4, 22],
            [14, 19, 21, 20, 8, 23, 12, 22, 4, 2, 10, 0, 6],
            [14, 16, 20, 22, 21, 10, 0, 12, 8, 6, 23, 2, 4],
            [18, 23, 22, 14, 2, 16, 10, 0, 12, 8, 6, 4],
            [20],
        ],
    ),
    (
        [
            [-1, 0, 4, 4, 0, 4, 4, 6, 10, 11, 11, 1],
            [-1, -1, 1, 4, 1, 4, 4, 9, 9, 11, 7, 1],
            [-1, -1, -1, 4, 2, 4, 5, 8, 6, 8, 8, 10],
            [-1, -1, -1, -1, 3, 4, 5, 6, 7, 8, 6, 10],
            [-1, -1, -1, -1, -1, 6, 4, 6, 4, 11, 11, 8],
            [-1, -1, -1, -1, -1, -1, 5, 6, 6, 10, 8, 10],
            [-1, -1, -1, -1, -1, -1, -1, 6, 7, 7, 9, 10],
            [-1, -1, -1, -1, -1, -1, -1, -1, 7, 10, 8, 10],
            [-1, -1, -1, -1, -1, -1, -1, -1, -1, 8, 9, 10],
            [-1, -1, -1, -1, -1, -1, -1, -1, -1, -1, 9, 10],
            [-1, -1, -1, -1, -1, -1, -1, -1, -1, -1, -1, 10],
            [11, 0, 0, 4, 9, 7, 7, 9, 9, 11, 9, -1],
        ],
        [
            [-1, -1, -1, -1, -1, -1, -1, -1, -1, -1, -1, -1],
            [1, -1, -1, -1, -1, -1, -1, -1, -1, -1, -1, -1],
            [2, 2, -1, -1, -1, -1, -1, -1, -1, -1, -1, -1],
            [1, 3, 3, -1, -1, -1, -1, -1, -1, -1, -1, -1],
            [2, 0, 4, 2, -1, -1, -1, -1, -1, -1, -1, -1],
            [1, 2, 5, 4, 5, -1, -1, -1, -1, -1, -1, -1],
            [1, 2, 6, 2, 3, 3, -1, -1, -1, -1, -1, -1],
            [1, 3, 3, 7, 5, 7, 5, -1, -1, -1, -1, -1],
            [2, 2, 8, 2, 5, 7, 5, 8, -1, -1, -1, -1],
            [8, 3, 3, 9, 3, 7, 5, 8, 9, -1, -1, -1],
            [10, 0, 4, 4, 7, 4, 7, 10, 10, 8, -1, -1],
            [11, 11, 1, 1, 6, 6, 8, 6, 9, 11, 0, -1],
        ],
        [
            [5, 3, 7, 21, 23, 9, 11, 22, 19, 17, 13, 15],
            [5, 7, 0, 11, 13, 15, 23, 21, 17, 9, 19, 22],
            [7, 11, 9, 13, 17, 2, 15, 0, 19, 23, 21, 22],
            [15, 4, 11, 19, 0, 9, 13, 17, 21, 2, 23, 22],
            [4, 6, 11, 0, 21, 15, 2, 19, 22, 17, 13, 23],
            [4, 15, 6, 17, 8, 0, 19, 21, 2, 22, 13, 23],
            [10, 8, 4, 15, 21, 6, 0, 17, 23, 19, 22, 2],
            [17, 21, 12, 19, 10, 8, 22, 6, 2, 0, 4, 23],
            [19, 21, 8, 14, 10, 23, 12, 22, 4, 2, 0, 6],
            [16, 23, 22, 2, 21, 0, 12, 4, 8, 14, 10, 6],
            [18, 16, 0, 23, 22, 14, 10, 6, 8, 12, 4, 2],
            [2, 0, 20, 8, 18, 16, 14, 10, 6, 12, 4],
        ],
    ),
]


def word(plan, chip, code):
    source = plan[code % 2][code // 2]
    to = [w for w in range(len(source)) if source[w] == chip]
    to = sorted(to, key=lambda w: (w > chip) * 100 + w)
    to = to + [NONE] * (4 - len(to))
    return code + 32 * (to[0] + 16 * (to[1] + 16 * (to[2] + 16 * to[3])))


def kernel(
    plan, chips,
    doc_ref, q_hbm, k_hbm, v_hbm, out_ref,
    q_ref, kv, acc, peak, total, give, give_at, take, take_at,
    load_sem, ring_send, ring_recv, mate_send, mate_recv, q_sem, side_send, side_recv,
):
    ctx, tp = lax.axis_index("ctx"), lax.axis_index("tp")
    z, core = ctx // 2, ctx % 2
    other = 1 - core
    odd = tp % 2
    shards = 2 * chips
    mate = (2 * z + other, tp)
    side = (ctx, tp + 1 - 2 * odd)
    order = plan[2]

    loads = []
    for kind in (1, 0):
        for part, hbm in enumerate((k_hbm, v_hbm)):
            half = hbm.at[pl.ds(pl.multiple_of(kind * SPAN + odd * BLK, BLK), BLK)]
            loads.append(
                pltpu.make_async_copy(half, kv.at[z, kind, part, core], load_sem.at[2 * kind + part])
            )
    loads.append(pltpu.make_async_copy(q_hbm, q_ref.at[:, 0], load_sem.at[4]))
    for copy in loads:
        copy.start()

    def by_chip(values):
        return functools.reduce(lambda a, i: jnp.where(z == i, values[i], a), range(1, chips), jnp.int32(values[0]))

    def chip(w):
        return (2 * w + core, tp)

    parents = [sorted({t[s][w] for t in plan[:2] for s in range(chips)} - {-1}) for w in range(chips)]
    targets = [sum(w in p for p in parents) for w in range(chips)]

    barrier = pltpu.get_barrier_semaphore()
    for neighbour in (mate, side):
        pl.semaphore_signal(barrier, inc=1, device_id=neighbour, device_id_type=MESH)

    def greet(w, left):
        @pl.when(lax.rem(left, 2) == 1)
        def _():
            pl.semaphore_signal(barrier, inc=1, device_id=chip(w), device_id_type=MESH)

        return lax.div(left, 2)

    lax.fori_loop(0, chips, greet, by_chip([sum(1 << p for p in ps) for ps in parents]))

    steps = max(map(len, order))
    words = [by_chip([word(plan, w, o[e]) if e < len(o) else 0 for w, o in enumerate(order)]) for e in range(steps)]
    own_words = [by_chip([word(plan, w, 2 * w + kind) for w in range(chips)]) for kind in range(2)]
    count = by_chip([len(o) for o in order])
    pl.semaphore_wait(barrier, by_chip(targets) + 2)

    def remote(src, dst, send_sem, recv_sem, device):
        return pltpu.make_async_remote_copy(
            src_ref=src, dst_ref=dst, send_sem=send_sem, recv_sem=recv_sem, device_id=device, device_id_type=MESH
        )

    def ring_copy(s, kind, j, device):
        piece = kv.at[s, kind, :, core]
        return remote(piece, piece, ring_send.at[s, kind, j], ring_recv.at[s, kind], device)

    def mate_copy(s, kind, who):
        piece = kv.at[s, kind, :, who]
        return remote(piece, piece, mate_send.at[s, kind], mate_recv.at[s, kind], mate)

    def side_copies(n):
        return [
            remote(give.at[n], take.at[n], side_send.at[n, 0], side_recv.at[n, 0], side),
            remote(give_at.at[n], take_at.at[n], side_send.at[n, 1], side_recv.at[n, 1], side),
        ]

    def each_child(w, act):
        code = lax.rem(w, 32)
        for j in range(4):
            to = lax.rem(lax.div(w, 32 * 16**j), 16)

            @pl.when(to < NONE)
            def _():
                act(ring_copy(lax.div(code, 2), lax.rem(code, 2), j, chip(to)))

    for kind in (1, 0):
        for copy in loads[2 * (1 - kind) : 2 * (1 - kind) + 2]:
            copy.wait()
        each_child(own_words[kind], lambda copy: copy.start())
        mate_copy(z, kind, core).start()
    loads[4].wait()
    q_copy = remote(q_ref.at[:, 0], q_ref.at[:, 1], q_sem.at[0], q_sem.at[1], side)
    q_copy.start()

    def key_block(s, kind, j):
        span = 2 * s + j
        return jnp.where(kind == 0, 2 * span, 2 * (2 * shards - 1 - span)) + odd

    def query_block(n):
        return jnp.where(n < 2, 2 * ctx, 2 * (2 * shards - 1 - ctx) - 2) + n

    def scored(n, s_chip, kind):
        k = kv[s_chip, kind, 0].reshape(2 * BLK, HD)
        q = q_ref[n].reshape(2 * BLK, HD)
        s = lax.dot_general(q, k, (((1,), (1,)), ((), ())), preferred_element_type=jnp.float32)
        return [s[:, j * BLK : (j + 1) * BLK] * SCALE for j in range(2)]

    def summed(weights, s_chip, kind):
        joined = jnp.concatenate([w.astype(jnp.bfloat16) for w in weights], axis=1)
        v = kv[s_chip, kind, 1].reshape(2 * BLK, HD)
        return jnp.dot(joined, v, preferred_element_type=jnp.float32)

    def own(n, kind):
        parts = scored(n, z, kind)
        q_block = query_block(n)
        row = lax.broadcasted_iota(jnp.int32, (2, BLK, BLK), 1).reshape(2 * BLK, BLK)
        inside = lax.broadcasted_iota(jnp.int32, (2 * BLK, BLK), 1) <= row
        for j in range(2):
            k_block = key_block(z, kind, j)
            same = doc_ref[k_block] == doc_ref[q_block]
            before = jnp.where(same & (k_block < q_block), 0.0, NEG)
            at_or_before = jnp.where(same & (k_block <= q_block), 0.0, NEG)
            parts[j] = parts[j] + jnp.where(inside, at_or_before, before)
        most = jnp.max(functools.reduce(jnp.maximum, parts), axis=1, keepdims=True)
        top = jnp.broadcast_to(jnp.maximum(most, FLOOR), (2 * BLK, HD))
        weights = [jnp.exp2(part - top) for part in parts]
        peak[n] = top
        total[n] = functools.reduce(jnp.add, weights)
        acc[n] = summed(weights, z, kind)

    def unit(n, s_chip, kind):
        parts = scored(n, s_chip, kind)
        q_block = query_block(n)
        for j in range(2):
            same = doc_ref[key_block(s_chip, kind, j)] == doc_ref[q_block]
            parts[j] = parts[j] + jnp.where(same, 0.0, NEG)
        old = peak[n]
        top = jnp.maximum(old, jnp.max(functools.reduce(jnp.maximum, parts), axis=1, keepdims=True))
        shrink = jnp.exp2(old - top)
        weights = [jnp.exp2(part - top) for part in parts]
        peak[n] = top
        total[n] = total[n] * shrink + functools.reduce(jnp.add, weights)
        acc[n] = acc[n] * shrink + summed(weights, s_chip, kind)

    def units(s, kind):
        low = (kind == 0) & (s < z)
        high = (kind == 1) | (s + z >= chips - 1)

        def pair(m, carry):
            for half in range(2):
                unit(2 * m + half, s, kind)
            return carry

        lax.fori_loop(jnp.where(low, 0, 1), jnp.where(high, 2, 1), pair, 0)

    def pick(e):
        w = functools.reduce(lambda a, i: jnp.where(e == i, words[i], a), range(1, steps), words[0])
        code = lax.rem(w, 32)
        return w, lax.div(code, 2), lax.rem(code, 2)

    def step(e, carry):
        @pl.when(e < count)
        def _():
            w, s, kind = pick(e)
            ring_copy(s, kind, 0, mate).wait_recv()
            each_child(w, lambda copy: copy.start())
            mate_copy(s, kind, core).start()

        @pl.when(e == 0)
        def _():
            q_copy.wait_recv()
            for kind in range(2):
                mate_copy(z, kind, other).wait_recv()

            def pair(m, carry):
                for half in range(2):
                    own(2 * m + half, m)
                return carry

            lax.fori_loop(0, 2, pair, 0)

            @pl.when(z + z >= chips - 1)
            def _():
                units(z, 0)

        @pl.when(e >= 1)
        def _():
            _, s, kind = pick(e - 1)
            mate_copy(s, kind, other).wait_recv()
            units(s, kind)

        return carry

    lax.fori_loop(0, count + 1, step, 0)

    def part(n, head):
        rows = pl.ds(head * BLK, BLK)
        mass = jnp.maximum(jnp.sum(total[n, rows], axis=1, keepdims=True), 1e-30)
        return acc[n, rows] / mass, peak[n, rows] + jnp.log(mass) * LOG2E

    for n in range(4):
        mixed, level = part(n, 1)
        give[n] = mixed.astype(jnp.bfloat16)
        give_at[n] = jnp.transpose(level)[:8]
        if n:
            for copy in side_copies(n - 1):
                copy.start()
    for copy in side_copies(3):
        copy.start()

    for n in range(4):
        mixed, level = part(n, 0)
        for copy in side_copies(n):
            copy.wait_recv()
        their_level = jnp.transpose(jnp.broadcast_to(take_at[n, 0:1], (BLK, HD)))
        top = jnp.maximum(level, their_level)
        ours, theirs = jnp.exp2(level - top), jnp.exp2(their_level - top)
        result = (mixed * ours + take[n].astype(jnp.float32) * theirs) / (ours + theirs)
        out_ref[n * BLK : (n + 1) * BLK] = result.astype(out_ref.dtype)

    q_copy.wait_send()
    for kind in range(2):
        each_child(own_words[kind], lambda copy: copy.wait_send())
        mate_copy(z, kind, core).wait_send()
    for n in range(4):
        for copy in side_copies(n):
            copy.wait_send()

    def drain(e, carry):
        w, s, kind = pick(e)
        each_child(w, lambda copy: copy.wait_send())
        mate_copy(s, kind, core).wait_send()
        return carry

    lax.fori_loop(0, count, drain, 0)


def call(ident, queries, keys, values, doc_blocks):
    rows = queries.shape[0]
    blocks = rows // BLK
    chips = lax.axis_size("ctx") // 2
    dma = pltpu.SemaphoreType.DMA
    return pl.pallas_call(
        functools.partial(kernel, PLANS[ident], chips),
        out_shape=pltpu.VMEM((rows, HD), jnp.bfloat16),
        in_specs=[pl.BlockSpec(memory_space=pltpu.SMEM)] + [pl.BlockSpec(memory_space=pl.ANY)] * 3,
        out_specs=pl.BlockSpec(memory_space=pltpu.VMEM),
        scratch_shapes=[
            pltpu.VMEM((blocks, 2, BLK, HD), jnp.bfloat16),
            pltpu.VMEM((chips, 2, 2, 2, BLK, HD), jnp.bfloat16),
            pltpu.VMEM((blocks, 2 * BLK, HD), jnp.float32),
            pltpu.VMEM((blocks, 2 * BLK, HD), jnp.float32),
            pltpu.VMEM((blocks, 2 * BLK, HD), jnp.float32),
            pltpu.VMEM((blocks, BLK, HD), jnp.bfloat16),
            pltpu.VMEM((blocks, 8, BLK), jnp.float32),
            pltpu.VMEM((blocks, BLK, HD), jnp.bfloat16),
            pltpu.VMEM((blocks, 8, BLK), jnp.float32),
            dma((5,)),
            dma((chips, 2, 4)),
            dma((chips, 2)),
            dma((chips, 2)),
            dma((chips, 2)),
            dma((2,)),
            dma((blocks, 2)),
            dma((blocks, 2)),
        ],
        compiler_params=pltpu.CompilerParams(collective_id=ident, has_side_effects=True),
    )(doc_blocks, queries.reshape(blocks, BLK, HD), keys, values)


def body(queries, keys, values, doc_blocks):
    starts = doc_blocks.shape[0] - LONGEST + 1
    whole = doc_blocks[:starts] == doc_blocks[LONGEST - 1 :]
    plans = lax.rem(lax.div(lax.iota(jnp.int32, starts), jnp.int32(STARTS)), jnp.int32(len(PLANS)))
    which = jnp.max(jnp.where(whole, plans, 0))
    return lax.switch(
        which, [functools.partial(call, i) for i in range(len(PLANS))], queries, keys, values, doc_blocks
    )


def solution(mesh):
    return jax.shard_map(
        body,
        mesh=mesh,
        in_specs=(P("ctx", "tp"), P("ctx", "tp"), P("ctx", "tp"), P()),
        out_specs=P("ctx", "tp"),
        check_vma=False,
    )
```

```python
import functools

import jax
import jax.numpy as jnp
from jax import lax
from jax.experimental import pallas as pl
from jax.experimental.pallas import tpu as pltpu
from jax.sharding import PartitionSpec as P

HD = 128
BLK = 128
SPAN = 256
LONGEST = 48
STARTS = 4
MESH = pl.DeviceIdType.MESH
LOG2E = 1.4426950408889634
SCALE = HD**-0.5 * LOG2E
NEG = -1e30
FLOOR = -1e29
NONE = 15

PLANS = [
    (
        [
            [-1, 0, 1, 2, 3, 7, 8, 10, 10, 11, 0, 1],
            [-1, -1, 3, 1, 3, 4, 4, 9, 9, 11, 11, 1],
            [-1, -1, -1, 2, 2, 6, 4, 6, 6, 10, 11, 3],
            [-1, -1, -1, -1, 3, 4, 4, 3, 7, 11, 11, 3],
            [-1, -1, -1, -1, -1, 6, 4, 5, 6, 7, 8, 10],
            [-1, -1, -1, -1, -1, -1, 5, 8, 6, 8, 8, 9],
            [-1, -1, -1, -1, -1, -1, -1, 6, 6, 8, 8, 9],
            [-1, -1, -1, -1, -1, -1, -1, -1, 7, 10, 8, 10],
            [-1, -1, -1, -1, -1, -1, -1, -1, -1, 8, 11, 9],
            [-1, -1, -1, -1, -1, -1, -1, -1, -1, -1, 9, 10],
            [-1, -1, -1, -1, -1, -1, -1, -1, -1, -1, -1, 10],
            [-1, -1, -1, -1, -1, -1, -1, -1, -1, -1, -1, -1],
        ],
        [
            [-1, -1, -1, -1, -1, -1, -1, -1, -1, -1, -1, -1],
            [1, -1, -1, -1, -1, -1, -1, -1, -1, -1, -1, -1],
            [2, 2, -1, -1, -1, -1, -1, -1, -1, -1, -1, -1],
            [2, 0, 3, -1, -1, -1, -1, -1, -1, -1, -1, -1],
            [1, 2, 4, 2, -1, -1, -1, -1, -1, -1, -1, -1],
            [2, 2, 3, 5, 2, -1, -1, -1, -1, -1, -1, -1],
            [2, 2, 5, 4, 5, 6, -1, -1, -1, -1, -1, -1],
            [5, 0, 5, 4, 5, 7, 7, -1, -1, -1, -1, -1],
            [8, 0, 1, 1, 0, 4, 8, 6, -1, -1, -1, -1],
            [8, 0, 5, 5, 5, 8, 5, 8, 9, -1, -1, -1],
            [10, 2, 0, 2, 6, 6, 10, 6, 9, 10, -1, -1],
            [11, 0, 1, 6, 6, 6, 8, 8, 11, 10, 11, -1],
        ],
        [
            [5, 3, 17, 21, 23, 19, 7, 15, 13, 9, 11],
            [5, 0, 9, 17, 23, 13, 19, 7, 11, 15, 21],
            [9, 7, 0, 13, 11, 15, 2, 21, 17, 19, 23],
            [4, 11, 2, 9, 13, 0, 19, 17, 15, 21, 23],
            [4, 6, 13, 2, 15, 21, 17, 19, 11, 0, 23],
            [13, 15, 8, 6, 19, 2, 21, 4, 0, 17, 23],
            [8, 10, 15, 17, 21, 4, 6, 23, 2, 0, 19],
            [12, 6, 19, 0, 17, 21, 23, 8, 4, 2, 10],
            [19, 12, 14, 23, 8, 0, 10, 21, 6, 2, 4],
            [16, 21, 12, 2, 23, 6, 10, 0, 14, 4, 8],
            [0, 18, 23, 12, 2, 14, 6, 4, 8, 16, 10],
            [2, 20, 6, 4, 0, 16, 18, 12, 14, 8, 10],
        ],
    ),
    (
        [
            [-1, 0, -1, -1, -1, -1, -1, -1, -1, -1, -1, -1],
            [-1, -1, 1, 1, 2, 4, 4, 8, 10, 10, 1, 10],
            [-1, -1, -1, 4, 2, 3, 5, 9, 9, 4, 9, 10],
            [-1, -1, -1, -1, 5, 3, 7, 5, 6, 7, 9, 10],
            [-1, -1, -1, -1, -1, 6, 4, 6, 7, 7, 9, 8],
            [-1, -1, -1, -1, -1, -1, 5, 5, 7, 10, 7, 10],
            [-1, -1, -1, -1, -1, -1, -1, 6, 9, 7, 8, 9],
            [-1, -1, -1, -1, -1, -1, -1, -1, 7, 10, 8, 10],
            [-1, -1, -1, -1, -1, -1, -1, -1, -1, 8, 8, 10],
            [-1, -1, -1, -1, -1, -1, -1, -1, -1, -1, 9, 10],
            [-1, -1, -1, -1, -1, -1, -1, -1, -1, -1, -1, 10],
            [-1, -1, -1, -1, -1, -1, -1, -1, -1, -1, 11, -1],
        ],
        [
            [-1, -1, -1, -1, -1, -1, -1, -1, -1, -1, -1, -1],
            [1, -1, -1, -1, -1, -1, -1, -1, -1, -1, -1, -1],
            [2, 2, -1, -1, -1, -1, -1, -1, -1, -1, -1, -1],
            [2, 3, 3, -1, -1, -1, -1, -1, -1, -1, -1, -1],
            [2, 2, 4, 2, -1, -1, -1, -1, -1, -1, -1, -1],
            [1, 3, 3, 5, 3, -1, -1, -1, -1, -1, -1, -1],
            [1, 6, 1, 1, 3, 6, -1, -1, -1, -1, -1, -1],
            [7, 0, 5, 2, 5, 7, 7, -1, -1, -1, -1, -1],
            [7, 8, 1, 1, 5, 6, 7, 8, -1, -1, -1, -1],
            [9, 0, 5, 5, 5, 8, 7, 8, 9, -1, -1, -1],
            [10, 0, 5, 5, 3, 10, 5, 8, 10, 10, -1, -1],
            [-1, -1, -1, -1, -1, -1, -1, -1, -1, -1, 11, -1],
        ],
        [
            [5, 3, 15, 7, 19, 13, 21, 9, 11, 17],
            [0, 5, 7, 13, 11, 17, 15, 9, 19, 21],
            [7, 2, 9, 11, 13, 15, 17, 21, 19],
            [11, 2, 4, 13, 21, 9, 17, 15, 19],
            [4, 6, 2, 11, 15, 19, 13, 17, 21],
            [6, 13, 15, 21, 19, 8, 4, 17, 2],
            [10, 8, 15, 17, 21, 6, 19, 2, 4],
            [17, 10, 12, 6, 19, 8, 21, 4, 2],
            [19, 14, 21, 10, 2, 4, 8, 6, 12],
            [21, 16, 4, 2, 12, 6, 14, 8, 10],
            [2, 23, 22, 16, 18, 14, 10, 4, 6, 8, 12],
            [20, 2, 16, 18, 14, 10, 12, 4, 8, 6],
        ],
    ),
    (
        [
            [-1, 0, 1, -1, -1, -1, -1, -1, -1, -1, -1, -1],
            [-1, -1, 1, -1, -1, -1, -1, -1, -1, -1, -1, -1],
            [-1, -1, -1, 2, 3, 4, 5, 8, 11, 11, 11, 2],
            [-1, -1, -1, -1, 3, 4, 7, 5, 5, 8, 7, 10],
            [-1, -1, -1, -1, -1, 4, 7, 5, 6, 7, 9, 6],
            [-1, -1, -1, -1, -1, -1, 5, 9, 9, 6, 7, 9],
            [-1, -1, -1, -1, -1, -1, -1, 6, 7, 6, 11, 9],
            [-1, -1, -1, -1, -1, -1, -1, -1, 11, 11, 11, 7],
            [-1, -1, -1, -1, -1, -1, -1, -1, -1, 10, 8, 10],
            [-1, -1, -1, -1, -1, -1, -1, -1, -1, -1, 11, 9],
            [-1, -1, -1, -1, -1, -1, -1, -1, -1, 10, -1, 10],
            [-1, -1, -1, -1, -1, -1, -1, -1, -1, 10, 11, -1],
        ],
        [
            [-1, -1, -1, -1, -1, -1, -1, -1, -1, -1, -1, -1],
            [1, -1, -1, -1, -1, -1, -1, -1, -1, -1, -1, -1],
            [2, 0, -1, -1, -1, -1, -1, -1, -1, -1, -1, -1],
            [2, 3, 3, -1, -1, -1, -1, -1, -1, -1, -1, -1],
            [1, 2, 4, 1, -1, -1, -1, -1, -1, -1, -1, -1],
            [1, 3, 1, 5, 3, -1, -1, -1, -1, -1, -1, -1],
            [4, 4, 1, 5, 6, 4, -1, -1, -1, -1, -1, -1],
            [7, 0, 3, 7, 3, 4, 5, -1, -1, -1, -1, -1],
            [8, 0, 1, 4, 7, 4, 5, 8, -1, -1, -1, -1],
            [9, 0, 3, 6, 5, 6, 9, 9, 9, -1, -1, -1],
            [-1, -1, -1, -1, -1, -1, -1, -1, -1, 10, -1, -1],
            [-1, -1, -1, -1, -1, -1, -1, -1, -1, 10, 11, -1],
        ],
        [
            [3, 5, 17, 7, 15, 19, 13, 9, 11],
            [7, 0, 9, 5, 11, 17, 13, 15, 19],
            [7, 2, 9, 0, 15, 11, 17, 19, 13],
            [4, 11, 15, 19, 9, 13, 17],
            [6, 13, 4, 11, 17, 15, 19],
            [8, 6, 13, 19, 4, 17, 15],
            [10, 19, 8, 6, 4, 17, 15],
            [17, 12, 19, 8, 6, 10, 4],
            [19, 12, 6, 4, 10, 8, 14],
            [21, 20, 12, 23, 22, 10, 16, 4, 8, 14, 6],
            [23, 22, 16, 4, 6, 14, 18, 12, 8, 10],
            [4, 14, 18, 20, 16, 12, 10, 8, 6],
        ],
    ),
    (
        [
            [-1, 0, 1, 0, -1, -1, -1, -1, -1, -1, -1, -1],
            [-1, -1, 3, 1, -1, -1, -1, -1, -1, -1, -1, -1],
            [-1, -1, -1, 2, -1, -1, -1, -1, -1, -1, -1, -1],
            [-1, -1, -1, -1, 5, 3, 4, 5, 7, 8, 11, 7],
            [-1, -1, -1, -1, -1, 4, 5, 5, 6, 8, 7, 10],
            [-1, -1, -1, -1, -1, -1, 5, 8, 6, 10, 8, 10],
            [-1, -1, -1, -1, -1, -1, -1, 8, 6, 10, 8, 10],
            [-1, -1, -1, -1, -1, -1, -1, -1, 7, 7, 8, 10],
            [-1, -1, -1, -1, -1, -1, -1, -1, -1, 11, 8, 10],
            [-1, -1, -1, -1, -1, -1, -1, -1, 9, -1, 9, 9],
            [-1, -1, -1, -1, -1, -1, -1, -1, 9, 10, -1, 10],
            [-1, -1, -1, -1, -1, -1, -1, -1, 10, 10, 11, -1],
        ],
        [
            [-1, -1, -1, -1, -1, -1, -1, -1, -1, -1, -1, -1],
            [1, -1, -1, -1, -1, -1, -1, -1, -1, -1, -1, -1],
            [2, 2, -1, -1, -1, -1, -1, -1, -1, -1, -1, -1],
            [1, 2, 3, -1, -1, -1, -1, -1, -1, -1, -1, -1],
            [2, 3, 4, 2, -1, -1, -1, -1, -1, -1, -1, -1],
            [1, 2, 5, 2, 3, -1, -1, -1, -1, -1, -1, -1],
            [2, 2, 6, 2, 5, 6, -1, -1, -1, -1, -1, -1],
            [7, 0, 3, 7, 6, 6, 7, -1, -1, -1, -1, -1],
            [8, 0, 0, 7, 7, 7, 7, 8, -1, -1, -1, -1],
            [-1, -1, -1, -1, -1, -1, -1, -1, 9, -1, -1, -1],
            [-1, -1, -1, -1, -1, -1, -1, -1, 10, 10, -1, -1],
            [-1, -1, -1, -1, -1, -1, -1, -1, 10, 10, 11, -1],
        ],
        [
            [3, 5, 17, 9, 15, 7, 13, 11],
            [0, 5, 7, 11, 17, 13, 9, 15],
            [7, 9, 11, 13, 0, 2, 17, 15],
            [2, 4, 0, 9, 15, 11, 13, 17],
            [6, 17, 13, 11, 15],
            [6, 8, 13, 17, 15],
            [10, 15, 8, 17, 6],
            [17, 6, 12, 8, 10],
            [19, 12, 18, 21, 14, 10, 23, 6, 22, 20, 8],
            [21, 20, 14, 23, 22, 12, 6, 16, 8, 10],
            [23, 22, 16, 18, 12, 14, 10, 8, 6],
            [18, 20, 16, 6, 12, 14, 10, 8],
        ],
    ),
    (
        [
            [-1, 0, 1, 0, 3, -1, -1, -1, -1, -1, -1, -1],
            [-1, -1, 1, 2, 2, -1, -1, -1, -1, -1, -1, -1],
            [-1, -1, -1, 2, 2, -1, -1, -1, -1, -1, -1, -1],
            [-1, -1, -1, -1, 3, -1, -1, -1, -1, -1, -1, -1],
            [-1, -1, -1, -1, -1, 4, 5, 8, 6, 8, 8, 9],
            [-1, -1, -1, -1, -1, -1, 5, 8, 6, 10, 8, 10],
            [-1, -1, -1, -1, -1, -1, -1, 6, 7, 10, 8, 10],
            [-1, -1, -1, -1, -1, -1, -1, -1, 11, 11, 11, 7],
            [-1, -1, -1, -1, -1, -1, -1, 8, -1, 8, 9, 10],
            [-1, -1, -1, -1, -1, -1, -1, 8, 9, -1, 11, 9],
            [-1, -1, -1, -1, -1, -1, -1, 10, 7, 8, -1, 10],
            [-1, -1, -1, -1, -1, -1, -1, 9, 9, 11, 9, -1],
        ],
        [
            [-1, -1, -1, -1, -1, -1, -1, -1, -1, -1, -1, -1],
            [1, -1, -1, -1, -1, -1, -1, -1, -1, -1, -1, -1],
            [2, 2, -1, -1, -1, -1, -1, -1, -1, -1, -1, -1],
            [1, 3, 3, -1, -1, -1, -1, -1, -1, -1, -1, -1],
            [2, 2, 4, 2, -1, -1, -1, -1, -1, -1, -1, -1],
            [5, 0, 5, 2, 3, -1, -1, -1, -1, -1, -1, -1],
            [5, 5, 5, 5, 3, 6, -1, -1, -1, -1, -1, -1],
            [7, 0, 3, 7, 5, 6, 7, -1, -1, -1, -1, -1],
            [-1, -1, -1, -1, -1, -1, -1, 8, -1, -1, -1, -1],
            [-1, -1, -1, -1, -1, -1, -1, 8, 9, -1, -1, -1],
            [-1, -1, -1, -1, -1, -1, -1, 9, 7, 10, -1, -1],
            [-1, -1, -1, -1, -1, -1, -1, 8, 10, 8, 11, -1],
        ],
        [
            [3, 5, 11, 7, 15, 9, 13],
            [7, 0, 5, 9, 11, 13, 15],
            [7, 2, 9, 11, 0, 13, 15],
            [4, 0, 15, 2, 9, 11, 13],
            [6, 4, 2, 0, 15, 11, 13],
            [8, 13, 15],
            [10, 8, 15],
            [12, 17, 16, 20, 19, 21, 18, 22, 10, 8, 23],
            [19, 18, 10, 12, 8, 23, 20, 22, 21, 14],
            [16, 21, 22, 8, 14, 10, 23, 12, 20],
            [23, 16, 22, 10, 12, 14, 18, 8],
            [14, 18, 20, 16, 10, 12, 8],
        ],
    ),
    (
        [
            [-1, 0, 0, 2, 0, 4, -1, -1, -1, -1, -1, -1],
            [-1, -1, 1, 2, 1, 4, -1, -1, -1, -1, -1, -1],
            [-1, -1, -1, 4, 2, 4, -1, -1, -1, -1, -1, -1],
            [-1, -1, -1, -1, 3, 4, -1, -1, -1, -1, -1, -1],
            [-1, -1, -1, -1, -1, 4, -1, -1, -1, -1, -1, -1],
            [-1, -1, -1, -1, -1, -1, 5, 6, 7, 7, 9, 8],
            [-1, -1, -1, -1, -1, -1, -1, 6, 7, 7, 9, 10],
            [-1, -1, -1, -1, -1, -1, 7, -1, 9, 7, 11, 9],
            [-1, -1, -1, -1, -1, -1, 7, 8, -1, 11, 8, 8],
            [-1, -1, -1, -1, -1, -1, 8, 6, 9, -1, 9, 10],
            [-1, -1, -1, -1, -1, -1, 7, 10, 7, 11, -1, 10],
            [-1, -1, -1, -1, -1, -1, 7, 10, 9, 10, 11, -1],
        ],
        [
            [-1, -1, -1, -1, -1, -1, -1, -1, -1, -1, -1, -1],
            [1, -1, -1, -1, -1, -1, -1, -1, -1, -1, -1, -1],
            [1, 2, -1, -1, -1, -1, -1, -1, -1, -1, -1, -1],
            [3, 0, 3, -1, -1, -1, -1, -1, -1, -1, -1, -1],
            [1, 4, 1, 1, -1, -1, -1, -1, -1, -1, -1, -1],
            [3, 3, 3, 5, 3, -1, -1, -1, -1, -1, -1, -1],
            [1, 6, 1, 4, 6, 6, -1, -1, -1, -1, -1, -1],
            [-1, -1, -1, -1, -1, -1, 7, -1, -1, -1, -1, -1],
            [-1, -1, -1, -1, -1, -1, 7, 8, -1, -1, -1, -1],
            [-1, -1, -1, -1, -1, -1, 7, 8, 9, -1, -1, -1],
            [-1, -1, -1, -1, -1, -1, 7, 10, 7, 8, -1, -1],
            [-1, -1, -1, -1, -1, -1, 7, 9, 9, 10, 11, -1],
        ],
        [
            [3, 7, 5, 9, 11, 13],
            [5, 0, 9, 13, 7, 11],
            [2, 7, 0, 9, 11, 13],
            [11, 4, 2, 9, 13, 0],
            [4, 2, 13, 6, 0, 11],
            [8, 4, 13, 2, 6, 0],
            [10, 15, 14, 17, 16, 18, 21, 20, 19, 22, 23],
            [12, 17, 16, 10, 21, 20, 19, 22, 23, 18],
            [19, 18, 12, 14, 10, 21, 20, 23, 22],
            [14, 23, 12, 22, 10, 16, 20, 21],
            [23, 22, 16, 18, 12, 14, 10],
            [16, 20, 14, 18, 10, 12],
        ],
    ),
    (
        [
            [-1, 0, 0, 1, 2, 4, 5, -1, -1, -1, -1, -1],
            [-1, -1, 1, 2, 3, 3, 4, -1, -1, -1, -1, -1],
            [-1, -1, -1, 2, 5, 3, 5, -1, -1, -1, -1, -1],
            [-1, -1, -1, -1, 5, 3, 5, -1, -1, -1, -1, -1],
            [-1, -1, -1, -1, -1, 4, 5, -1, -1, -1, -1, -1],
            [-1, -1, -1, -1, -1, -1, 5, -1, -1, -1, -1, -1],
            [-1, -1, -1, -1, -1, 6, -1, 6, 9, 6, 9, 9],
            [-1, -1, -1, -1, -1, 6, 7, -1, 7, 8, 9, 6],
            [-1, -1, -1, -1, -1, 7, 7, 9, -1, 8, 9, 9],
            [-1, -1, -1, -1, -1, 6, 10, 6, 10, -1, 9, 9],
            [-1, -1, -1, -1, -1, 7, 7, 8, 10, 11, -1, 10],
            [-1, -1, -1, -1, -1, 11, 5, 9, 9, 11, 11, -1],
        ],
        [
            [-1, -1, -1, -1, -1, -1, -1, -1, -1, -1, -1, -1],
            [1, -1, -1, -1, -1, -1, -1, -1, -1, -1, -1, -1],
            [1, 2, -1, -1, -1, -1, -1, -1, -1, -1, -1, -1],
            [3, 0, 3, -1, -1, -1, -1, -1, -1, -1, -1, -1],
            [4, 4, 1, 4, -1, -1, -1, -1, -1, -1, -1, -1],
            [4, 4, 4, 4, 5, -1, -1, -1, -1, -1, -1, -1],
            [-1, -1, -1, -1, -1, 6, -1, -1, -1, -1, -1, -1],
            [-1, -1, -1, -1, -1, 6, 7, -1, -1, -1, -1, -1],
            [-1, -1, -1, -1, -1, 6, 7, 8, -1, -1, -1, -1],
            [-1, -1, -1, -1, -1, 6, 9, 6, 7, -1, -1, -1],
            [-1, -1, -1, -1, -1, 6, 10, 6, 7, 6, -1, -1],
            [-1, -1, -1, -1, -1, 11, 5, 8, 10, 10, 11, -1],
        ],
        [
            [3, 7, 9, 5, 11],
            [0, 5, 9, 7, 11],
            [0, 2, 7, 11, 9],
            [4, 0, 2, 9, 11],
            [11, 0, 6, 4, 2],
            [6, 8, 13, 12, 4, 15, 14, 23, 19, 22, 21, 0, 17, 2, 16, 18, 20],
            [10, 15, 14, 19, 6, 21, 8, 17, 4, 18, 23, 16, 22, 2, 20, 0],
            [17, 12, 16, 19, 20, 21, 22, 18, 23],
            [14, 20, 18, 23, 22, 19, 12, 21],
            [16, 22, 12, 14, 23, 20, 21],
            [18, 23, 22, 16, 12, 14],
            [18, 20, 16, 14, 12],
        ],
    ),
    (
        [
            [-1, 0, 3, 0, 0, 4, 5, 5, -1, -1, -1, -1],
            [-1, -1, 3, 1, 3, 1, 5, 6, -1, -1, -1, -1],
            [-1, -1, -1, 2, 3, 3, 5, 6, -1, -1, -1, -1],
            [-1, -1, -1, -1, 3, 4, 5, 6, -1, -1, -1, -1],
            [-1, -1, -1, -1, -1, 4, 7, 5, -1, -1, -1, -1],
            [-1, -1, -1, -1, -1, -1, 5, 5, -1, -1, -1, -1],
            [-1, -1, -1, -1, -1, -1, -1, 6, -1, -1, -1, -1],
            [-1, -1, -1, -1, 6, 4, 7, -1, 7, 6, 8, 10],
            [-1, -1, -1, -1, 6, 4, 8, 6, -1, 8, 9, 9],
            [-1, -1, -1, -1, 11, 4, 7, 8, 9, -1, 11, 9],
            [-1, -1, -1, -1, 11, 6, 10, 8, 11, 11, -1, 10],
            [-1, -1, -1, -1, 11, 4, 8, 8, 11, 10, 11, -1],
        ],
        [
            [-1, -1, -1, -1, -1, -1, -1, -1, -1, -1, -1, -1],
            [1, -1, -1, -1, -1, -1, -1, -1, -1, -1, -1, -1],
            [1, 2, -1, -1, -1, -1, -1, -1, -1, -1, -1, -1],
            [1, 3, 1, -1, -1, -1, -1, -1, -1, -1, -1, -1],
            [1, 4, 4, 4, -1, -1, -1, -1, -1, -1, -1, -1],
            [-1, -1, -1, -1, 5, -1, -1, -1, -1, -1, -1, -1],
            [-1, -1, -1, -1, 6, 6, -1, -1, -1, -1, -1, -1],
            [-1, -1, -1, -1, 5, 6, 7, -1, -1, -1, -1, -1],
            [-1, -1, -1, -1, 5, 6, 8, 6, -1, -1, -1, -1],
            [-1, -1, -1, -1, 6, 6, 8, 6, 9, -1, -1, -1],
            [-1, -1, -1, -1, 5, 6, 10, 8, 6, 8, -1, -1],
            [-1, -1, -1, -1, 11, 4, 7, 10, 10, 8, 11, -1],
        ],
        [
            [3, 5, 7, 9],
            [5, 7, 0, 9],
            [9, 2, 7, 0],
            [4, 2, 9, 0],
            [6, 4, 11, 13, 0, 23, 14, 22, 2, 16, 18, 15, 20, 17, 19, 21],
            [8, 13, 4, 2, 6, 15, 17, 0, 21, 23, 20, 14, 22, 19, 16, 18],
            [10, 15, 14, 17, 16, 21, 4, 20, 2, 19, 6, 8, 22, 23, 0, 18],
            [10, 12, 8, 17, 23, 16, 18, 4, 22, 2, 19, 20, 6, 21, 0],
            [14, 19, 18, 22, 23, 20, 21],
            [16, 14, 20, 22, 23, 21],
            [23, 22, 14, 18, 16],
            [18, 20, 16, 14],
        ],
    ),
    (
        [
            [-1, 0, 1, 4, 0, 4, 4, 6, 5, -1, -1, -1],
            [-1, -1, 3, 1, 1, 6, 4, 6, 7, -1, -1, -1],
            [-1, -1, -1, 2, 3, 6, 4, 6, 7, -1, -1, -1],
            [-1, -1, -1, -1, 3, 4, 7, 5, 7, -1, -1, -1],
            [-1, -1, -1, -1, -1, 6, 4, 6, 7, -1, -1, -1],
            [-1, -1, -1, -1, -1, -1, 5, 5, 7, -1, -1, -1],
            [-1, -1, -1, -1, -1, -1, -1, 8, 6, -1, -1, -1],
            [-1, -1, -1, -1, -1, -1, -1, -1, 7, -1, -1, -1],
            [-1, -1, -1, 11, 5, 6, 8, 8, -1, 11, 8, 10],
            [-1, -1, -1, 10, 3, 6, 7, 8, 9, -1, 9, 10],
            [-1, -1, -1, 11, 3, 6, 8, 9, 10, 11, -1, 10],
            [-1, -1, -1, 11, 3, 4, 7, 9, 9, 11, 11, -1],
        ],
        [
            [-1, -1, -1, -1, -1, -1, -1, -1, -1, -1, -1, -1],
            [1, -1, -1, -1, -1, -1, -1, -1, -1, -1, -1, -1],
            [1, 2, -1, -1, -1, -1, -1, -1, -1, -1, -1, -1],
            [1, 3, 3, -1, -1, -1, -1, -1, -1, -1, -1, -1],
            [-1, -1, -1, 4, -1, -1, -1, -1, -1, -1, -1, -1],
            [-1, -1, -1, 4, 5, -1, -1, -1, -1, -1, -1, -1],
            [-1, -1, -1, 6, 5, 6, -1, -1, -1, -1, -1, -1],
            [-1, -1, -1, 5, 5, 6, 7, -1, -1, -1, -1, -1],
            [-1, -1, -1, 5, 3, 8, 5, 6, -1, -1, -1, -1],
            [-1, -1, -1, 6, 6, 6, 8, 6, 9, -1, -1, -1],
            [-1, -1, -1, 10, 3, 4, 8, 9, 10, 8, -1, -1],
            [-1, -1, -1, 11, 5, 3, 5, 9, 10, 10, 11, -1],
        ],
        [
            [3, 5, 7],
            [5, 7, 0],
            [7, 2, 0],
            [4, 9, 2, 13, 11, 21, 23, 22, 17, 0, 20, 15, 18, 19, 16],
            [6, 4, 11, 2, 0, 13, 21, 15, 22, 17, 19, 20, 16, 23, 18],
            [13, 6, 17, 8, 15, 16, 0, 4, 23, 21, 19, 2, 22, 20, 18],
            [8, 15, 10, 16, 4, 19, 2, 21, 17, 20, 0, 18, 6, 22, 23],
            [16, 10, 18, 8, 6, 4, 19, 22, 12, 2, 21, 23, 17, 20, 0],
            [19, 18, 21, 20, 12, 14, 23, 10, 22, 8, 6, 0, 4, 2],
            [22, 21, 23, 20, 16],
            [23, 16, 18, 22],
            [20, 16, 18],
        ],
    ),
    (
        [
            [-1, 2, 0, 2, 2, 3, 5, 4, 9, 2, -1, -1],
            [-1, -1, 1, 4, 2, 6, 4, 6, 9, 2, -1, -1],
            [-1, -1, -1, 4, 2, 4, 5, 4, 7, 7, -1, -1],
            [-1, -1, -1, -1, 3, 4, 4, 6, 6, 8, -1, -1],
            [-1, -1, -1, -1, -1, 4, 7, 4, 7, 8, -1, -1],
            [-1, -1, -1, -1, -1, -1, 5, 8, 6, 8, -1, -1],
            [-1, -1, -1, -1, -1, -1, -1, 6, 7, 7, -1, -1],
            [-1, -1, -1, -1, -1, -1, -1, -1, 7, 7, -1, -1],
            [-1, -1, -1, -1, -1, -1, -1, -1, -1, 8, -1, -1],
            [-1, -1, 10, 2, 2, 6, 7, 8, 9, -1, 9, 9],
            [-1, -1, 11, 6, 5, 6, 10, 8, 9, 10, -1, 10],
            [-1, -1, 11, 2, 2, 4, 7, 9, 9, 11, 9, -1],
        ],
        [
            [-1, -1, -1, -1, -1, -1, -1, -1, -1, -1, -1, -1],
            [1, -1, -1, -1, -1, -1, -1, -1, -1, -1, -1, -1],
            [2, 2, -1, -1, -1, -1, -1, -1, -1, -1, -1, -1],
            [-1, -1, 3, -1, -1, -1, -1, -1, -1, -1, -1, -1],
            [-1, -1, 4, 2, -1, -1, -1, -1, -1, -1, -1, -1],
            [-1, -1, 3, 4, 5, -1, -1, -1, -1, -1, -1, -1],
            [-1, -1, 3, 6, 6, 4, -1, -1, -1, -1, -1, -1],
            [-1, -1, 3, 6, 3, 6, 7, -1, -1, -1, -1, -1],
            [-1, -1, 4, 4, 8, 4, 7, 8, -1, -1, -1, -1],
            [-1, -1, 9, 2, 3, 6, 7, 9, 7, -1, -1, -1],
            [-1, -1, 9, 2, 5, 7, 5, 9, 9, 10, -1, -1],
            [-1, -1, 11, 2, 3, 7, 7, 9, 9, 11, 9, -1],
        ],
        [
            [3, 5],
            [5, 0],
            [7, 2, 0, 9, 19, 23, 13, 22, 11, 21, 17, 18, 15, 20],
            [13, 11, 0, 15, 9, 4, 19, 17, 23, 2, 22, 20, 21, 18],
            [6, 11, 4, 13, 17, 2, 0, 15, 22, 19, 23, 20, 18, 21],
            [8, 6, 4, 15, 13, 17, 0, 20, 21, 19, 2, 23, 22, 18],
            [10, 15, 6, 20, 17, 8, 19, 2, 4, 18, 0, 23, 21, 22],
            [17, 8, 19, 12, 21, 18, 4, 6, 23, 10, 22, 0, 20, 2],
            [14, 18, 10, 21, 8, 19, 20, 12, 23, 6, 4, 22, 2, 0],
            [21, 14, 16, 20, 23, 22, 2, 0, 12, 10, 8, 4, 6],
            [18, 23, 22],
            [18, 20],
        ],
    ),
    (
        [
            [-1, 2, 0, 4, 2, 4, 8, 8, 10, 8, 0, -1],
            [-1, -1, 3, 4, 1, 6, 4, 6, 7, 7, 8, -1],
            [-1, -1, -1, 4, 2, 7, 4, 6, 7, 7, 9, -1],
            [-1, -1, -1, -1, 5, 6, 3, 6, 9, 7, 9, -1],
            [-1, -1, -1, -1, -1, 4, 5, 9, 9, 6, 9, -1],
            [-1, -1, -1, -1, -1, -1, 7, 5, 9, 7, 9, -1],
            [-1, -1, -1, -1, -1, -1, -1, 8, 6, 10, 8, -1],
            [-1, -1, -1, -1, -1, -1, -1, -1, 7, 8, 9, -1],
            [-1, -1, -1, -1, -1, -1, -1, -1, -1, 8, 9, -1],
            [-1, -1, -1, -1, -1, -1, -1, -1, -1, -1, 9, -1],
            [-1, 10, 1, 2, 5, 7, 5, 10, 7, 10, -1, 10],
            [-1, 11, 1, 1, 2, 3, 7, 9, 11, 11, 11, -1],
        ],
        [
            [-1, -1, -1, -1, -1, -1, -1, -1, -1, -1, -1, -1],
            [1, -1, -1, -1, -1, -1, -1, -1, -1, -1, -1, -1],
            [-1, 2, -1, -1, -1, -1, -1, -1, -1, -1, -1, -1],
            [-1, 2, 3, -1, -1, -1, -1, -1, -1, -1, -1, -1],
            [-1, 2, 4, 4, -1, -1, -1, -1, -1, -1, -1, -1],
            [-1, 3, 3, 5, 3, -1, -1, -1, -1, -1, -1, -1],
            [-1, 2, 6, 2, 3, 3, -1, -1, -1, -1, -1, -1],
            [-1, 2, 7, 5, 5, 7, 5, -1, -1, -1, -1, -1],
            [-1, 3, 3, 7, 7, 6, 4, 8, -1, -1, -1, -1],
            [-1, 8, 1, 4, 8, 6, 7, 8, 9, -1, -1, -1],
            [-1, 3, 3, 10, 3, 4, 7, 8, 10, 8, -1, -1],
            [-1, 10, 1, 4, 11, 6, 4, 8, 10, 1, 11, -1],
        ],
        [
            [3],
            [5, 7, 20, 9, 0, 22, 11, 13, 19, 23, 21, 15, 17],
            [7, 9, 0, 13, 15, 11, 20, 21, 22, 17, 19, 2, 23],
            [9, 11, 21, 4, 17, 2, 13, 15, 23, 22, 19, 20, 0],
            [4, 2, 17, 23, 19, 0, 11, 15, 21, 6, 13, 20, 22],
            [8, 15, 6, 20, 2, 4, 0, 19, 13, 21, 17, 23, 22],
            [6, 4, 8, 2, 10, 15, 19, 17, 0, 23, 21, 20, 22],
            [17, 10, 20, 6, 19, 4, 21, 12, 2, 22, 0, 23, 8],
            [19, 21, 12, 22, 14, 0, 20, 23, 10, 4, 2, 8, 6],
            [16, 20, 22, 21, 10, 8, 6, 14, 4, 0, 23, 2, 12],
            [18, 0, 23, 16, 22, 12, 10, 8, 6, 14, 4, 2],
            [20],
        ],
    ),
    (
        [
            [-1, 0, 1, 2, 2, 3, 8, 8, 10, 8, 0, 1],
            [-1, -1, 3, 1, 5, 3, 5, 5, 7, 10, 11, 1],
            [-1, -1, -1, 5, 2, 4, 5, 5, 10, 10, 11, 2],
            [-1, -1, -1, -1, 3, 6, 4, 6, 7, 7, 6, 10],
            [-1, -1, -1, -1, -1, 4, 5, 6, 7, 6, 9, 9],
            [-1, -1, -1, -1, -1, -1, 5, 6, 6, 7, 9, 9],
            [-1, -1, -1, -1, -1, -1, -1, 6, 6, 8, 9, 10],
            [-1, -1, -1, -1, -1, -1, -1, -1, 7, 7, 11, 9],
            [-1, -1, -1, -1, -1, -1, -1, -1, -1, 8, 11, 9],
            [-1, -1, -1, -1, -1, -1, -1, -1, -1, -1, 9, 10],
            [-1, -1, -1, -1, -1, -1, -1, -1, -1, -1, -1, 10],
            [10, 11, 1, 1, 6, 6, 7, 11, 10, 8, 11, -1],
        ],
        [
            [-1, -1, -1, -1, -1, -1, -1, -1, -1, -1, -1, -1],
            [1, -1, -1, -1, -1, -1, -1, -1, -1, -1, -1, -1],
            [1, 2, -1, -1, -1, -1, -1, -1, -1, -1, -1, -1],
            [1, 3, 3, -1, -1, -1, -1, -1, -1, -1, -1, -1],
            [1, 3, 1, 4, -1, -1, -1, -1, -1, -1, -1, -1],
            [2, 2, 3, 5, 5, -1, -1, -1, -1, -1, -1, -1],
            [1, 4, 3, 4, 6, 6, -1, -1, -1, -1, -1, -1],
            [3, 0, 4, 7, 3, 4, 5, -1, -1, -1, -1, -1],
            [8, 0, 3, 4, 6, 3, 8, 6, -1, -1, -1, -1],
            [9, 0, 1, 5, 5, 6, 7, 9, 9, -1, -1, -1],
            [9, 10, 3, 1, 3, 6, 7, 10, 7, 10, -1, -1],
            [1, 11, 1, 2, 5, 7, 7, 10, 9, 10, 11, -1],
        ],
        [
            [3, 17, 7, 19, 5, 15, 9, 21, 11, 23, 22, 13],
            [7, 0, 5, 9, 21, 23, 22, 13, 17, 19, 11, 15],
            [7, 0, 11, 2, 9, 23, 15, 22, 13, 17, 19, 21],
            [9, 11, 2, 15, 0, 13, 17, 21, 4, 19, 22, 23],
            [6, 11, 13, 4, 17, 15, 2, 0, 19, 21, 22, 23],
            [8, 13, 2, 6, 4, 19, 15, 21, 0, 23, 17, 22],
            [10, 17, 6, 8, 19, 21, 2, 22, 0, 4, 23, 15],
            [12, 19, 10, 21, 17, 22, 6, 23, 8, 0, 2, 4],
            [14, 19, 12, 10, 0, 22, 21, 4, 6, 23, 8, 2],
            [14, 16, 21, 12, 10, 23, 2, 8, 4, 0, 6, 22],
            [0, 23, 18, 22, 2, 4, 6, 14, 12, 16, 10, 8],
            [2, 4, 20, 0, 14, 16, 18, 10, 6, 12, 8],
        ],
    ),
]


def word(plan, chip, code):
    source = plan[code % 2][code // 2]
    to = [w for w in range(len(source)) if source[w] == chip]
    to = sorted(to, key=lambda w: (w > chip) * 100 + w)
    to = to + [NONE] * (4 - len(to))
    return code + 32 * (to[0] + 16 * (to[1] + 16 * (to[2] + 16 * to[3])))


def kernel(
    plan, chips,
    q_hbm, k_hbm, v_hbm, doc_hbm, out_ref,
    doc_ref, q_ref, kv, acc, peak, total, give, give_at, take, take_at,
    load_sem, ring_send, ring_recv, mate_send, mate_recv, q_sem, side_send, side_recv,
):
    ctx, tp = lax.axis_index("ctx"), lax.axis_index("tp")
    z, core = ctx // 2, ctx % 2
    other = 1 - core
    odd = tp % 2
    shards = 2 * chips
    mate = (2 * z + other, tp)
    side = (ctx, tp + 1 - 2 * odd)
    order = plan[2]
    low_steps = [max([i + 2 for i, o in enumerate(took) if o % 2 == 0 and o // 2 < w] + [1]) for w, took in enumerate(order)]

    loads = []
    for kind in (1, 0):
        for part, hbm in enumerate((k_hbm, v_hbm)):
            half = hbm.at[pl.ds(pl.multiple_of(kind * SPAN + odd * BLK, BLK), BLK)]
            loads.append(
                pltpu.make_async_copy(half, kv.at[z, kind, part, core], load_sem.at[2 * kind + part])
            )
    loads.append(pltpu.make_async_copy(q_hbm, q_ref.at[:, 0], load_sem.at[4]))
    loads.append(pltpu.make_async_copy(doc_hbm, doc_ref, load_sem.at[5]))
    for copy in loads:
        copy.start()

    def by_chip(values):
        return functools.reduce(lambda a, i: jnp.where(z == i, values[i], a), range(1, chips), jnp.int32(values[0]))

    def chip(w):
        return (2 * w + core, tp)

    parents = [sorted({t[s][w] for t in plan[:2] for s in range(chips)} - {-1}) for w in range(chips)]
    targets = [sum(w in p for p in parents) for w in range(chips)]

    barrier = pltpu.get_barrier_semaphore()
    for neighbour in (mate, side):
        pl.semaphore_signal(barrier, inc=1, device_id=neighbour, device_id_type=MESH)

    def greet(w, left):
        @pl.when(lax.rem(left, 2) == 1)
        def _():
            pl.semaphore_signal(barrier, inc=1, device_id=chip(w), device_id_type=MESH)

        return lax.div(left, 2)

    lax.fori_loop(0, chips, greet, by_chip([sum(1 << p for p in ps) for ps in parents]))

    steps = max(map(len, order))
    words = [by_chip([word(plan, w, o[e]) if e < len(o) else 0 for w, o in enumerate(order)]) for e in range(steps)]
    own_words = [by_chip([word(plan, w, 2 * w + kind) for w in range(chips)]) for kind in range(2)]
    count = by_chip([len(o) for o in order])
    pl.semaphore_wait(barrier, by_chip(targets) + 2)

    def remote(src, dst, send_sem, recv_sem, device):
        return pltpu.make_async_remote_copy(
            src_ref=src, dst_ref=dst, send_sem=send_sem, recv_sem=recv_sem, device_id=device, device_id_type=MESH
        )

    def ring_copy(s, kind, j, device):
        piece = kv.at[s, kind, :, core]
        return remote(piece, piece, ring_send.at[s, kind, j], ring_recv.at[s, kind], device)

    def mate_copy(s, kind, who):
        piece = kv.at[s, kind, :, who]
        return remote(piece, piece, mate_send.at[s, kind], mate_recv.at[s, kind], mate)

    def side_copies(n):
        return [
            remote(give.at[n], take.at[n], side_send.at[n, 0], side_recv.at[n, 0], side),
            remote(give_at.at[n], take_at.at[n], side_send.at[n, 1], side_recv.at[n, 1], side),
        ]

    def each_child(w, act):
        code = lax.rem(w, 32)
        for j in range(4):
            to = lax.rem(lax.div(w, 32 * 16**j), 16)

            @pl.when(to < NONE)
            def _():
                act(ring_copy(lax.div(code, 2), lax.rem(code, 2), j, chip(to)))

    for kind in (1, 0):
        for copy in loads[2 * (1 - kind) : 2 * (1 - kind) + 2]:
            copy.wait()
        each_child(own_words[kind], lambda copy: copy.start())
        mate_copy(z, kind, core).start()
    loads[4].wait()
    loads[5].wait()
    q_copy = remote(q_ref.at[:, 0], q_ref.at[:, 1], q_sem.at[0], q_sem.at[1], side)
    q_copy.start()

    def key_block(s, kind, j):
        span = 2 * s + j
        return jnp.where(kind == 0, 2 * span, 2 * (2 * shards - 1 - span)) + odd

    def query_block(n):
        return jnp.where(n < 2, 2 * ctx, 2 * (2 * shards - 1 - ctx) - 2) + n

    def scored(n, s_chip, kind):
        k = kv[s_chip, kind, 0].reshape(2 * BLK, HD)
        q = q_ref[n].reshape(2 * BLK, HD)
        s = lax.dot_general(q, k, (((1,), (1,)), ((), ())), preferred_element_type=jnp.float32)
        return [s[:, j * BLK : (j + 1) * BLK] * SCALE for j in range(2)]

    def summed(weights, s_chip, kind):
        joined = jnp.concatenate([w.astype(jnp.bfloat16) for w in weights], axis=1)
        v = kv[s_chip, kind, 1].reshape(2 * BLK, HD)
        return jnp.dot(joined, v, preferred_element_type=jnp.float32)

    def own(n, kind):
        parts = scored(n, z, kind)
        q_block = query_block(n)
        row = lax.broadcasted_iota(jnp.int32, (2, BLK, BLK), 1).reshape(2 * BLK, BLK)
        inside = lax.broadcasted_iota(jnp.int32, (2 * BLK, BLK), 1) <= row
        for j in range(2):
            k_block = key_block(z, kind, j)
            same = doc_ref[k_block] == doc_ref[q_block]
            before = jnp.where(same & (k_block < q_block), 0.0, NEG)
            at_or_before = jnp.where(same & (k_block <= q_block), 0.0, NEG)
            parts[j] = parts[j] + jnp.where(inside, at_or_before, before)
        most = jnp.max(functools.reduce(jnp.maximum, parts), axis=1, keepdims=True)
        top = jnp.broadcast_to(jnp.maximum(most, FLOOR), (2 * BLK, HD))
        weights = [jnp.exp2(part - top) for part in parts]
        peak[n] = top
        total[n] = functools.reduce(jnp.add, weights)
        acc[n] = summed(weights, z, kind)

    def unit(n, s_chip, kind):
        parts = scored(n, s_chip, kind)
        q_block = query_block(n)
        for j in range(2):
            same = doc_ref[key_block(s_chip, kind, j)] == doc_ref[q_block]
            parts[j] = parts[j] + jnp.where(same, 0.0, NEG)
        old = peak[n]
        top = jnp.maximum(old, jnp.max(functools.reduce(jnp.maximum, parts), axis=1, keepdims=True))
        shrink = jnp.exp2(old - top)
        weights = [jnp.exp2(part - top) for part in parts]
        peak[n] = top
        total[n] = total[n] * shrink + functools.reduce(jnp.add, weights)
        acc[n] = acc[n] * shrink + summed(weights, s_chip, kind)

    def units(s, kind):
        low = (kind == 0) & (s < z)
        high = (kind == 1) | (s + z >= chips - 1)

        def pair(m, carry):
            for half in range(2):
                unit(2 * m + half, s, kind)
            return carry

        lax.fori_loop(jnp.where(low, 0, 1), jnp.where(high, 2, 1), pair, 0)

    def pick(e):
        w = functools.reduce(lambda a, i: jnp.where(e == i, words[i], a), range(1, steps), words[0])
        code = lax.rem(w, 32)
        return w, lax.div(code, 2), lax.rem(code, 2)

    def part(n, head):
        rows = pl.ds(head * BLK, BLK)
        mass = jnp.maximum(jnp.sum(total[n, rows], axis=1, keepdims=True), 1e-30)
        return acc[n, rows] / mass, peak[n, rows] + jnp.log(mass) * LOG2E

    def hand_over(first):
        for n in (first, first + 1):
            mixed, level = part(n, 1)
            give[n] = mixed.astype(jnp.bfloat16)
            give_at[n] = jnp.transpose(level)[:8]
            if n > first:
                for copy in side_copies(first):
                    copy.start()
        for copy in side_copies(first + 1):
            copy.start()

    low_done = by_chip(low_steps)

    def step(e, carry):
        @pl.when(e < count)
        def _():
            w, s, kind = pick(e)
            ring_copy(s, kind, 0, mate).wait_recv()
            each_child(w, lambda copy: copy.start())
            mate_copy(s, kind, core).start()

        @pl.when(e == 0)
        def _():
            q_copy.wait_recv()
            for kind in range(2):
                mate_copy(z, kind, other).wait_recv()

            def pair(m, carry):
                for half in range(2):
                    own(2 * m + half, m)
                return carry

            lax.fori_loop(0, 2, pair, 0)

            @pl.when(z + z >= chips - 1)
            def _():
                units(z, 0)

        @pl.when(e >= 1)
        def _():
            _, s, kind = pick(e - 1)
            mate_copy(s, kind, other).wait_recv()
            units(s, kind)

        @pl.when(e == low_done - 1)
        def _():
            hand_over(0)

        return carry

    lax.fori_loop(0, count + 1, step, 0)
    hand_over(2)

    for n in range(4):
        mixed, level = part(n, 0)
        for copy in side_copies(n):
            copy.wait_recv()
        their_level = jnp.transpose(jnp.broadcast_to(take_at[n, 0:1], (BLK, HD)))
        top = jnp.maximum(level, their_level)
        ours, theirs = jnp.exp2(level - top), jnp.exp2(their_level - top)
        result = (mixed * ours + take[n].astype(jnp.float32) * theirs) / (ours + theirs)
        out_ref[n * BLK : (n + 1) * BLK] = result.astype(out_ref.dtype)

    q_copy.wait_send()
    for kind in range(2):
        each_child(own_words[kind], lambda copy: copy.wait_send())
        mate_copy(z, kind, core).wait_send()
    for n in range(4):
        for copy in side_copies(n):
            copy.wait_send()

    def drain(e, carry):
        w, s, kind = pick(e)
        each_child(w, lambda copy: copy.wait_send())
        mate_copy(s, kind, core).wait_send()
        return carry

    lax.fori_loop(0, count, drain, 0)


def call(ident, queries, keys, values, doc_blocks):
    rows = queries.shape[0]
    blocks = rows // BLK
    chips = lax.axis_size("ctx") // 2
    dma = pltpu.SemaphoreType.DMA
    return pl.pallas_call(
        functools.partial(kernel, PLANS[ident], chips),
        out_shape=pltpu.VMEM((rows, HD), jnp.bfloat16),
        in_specs=[pl.BlockSpec(memory_space=pl.ANY)] * 3 + [pl.BlockSpec(memory_space=pltpu.HBM)],
        out_specs=pl.BlockSpec(memory_space=pltpu.VMEM),
        scratch_shapes=[
            pltpu.SMEM(doc_blocks.shape, jnp.int32),
            pltpu.VMEM((blocks, 2, BLK, HD), jnp.bfloat16),
            pltpu.VMEM((chips, 2, 2, 2, BLK, HD), jnp.bfloat16),
            pltpu.VMEM((blocks, 2 * BLK, HD), jnp.float32),
            pltpu.VMEM((blocks, 2 * BLK, HD), jnp.float32),
            pltpu.VMEM((blocks, 2 * BLK, HD), jnp.float32),
            pltpu.VMEM((blocks, BLK, HD), jnp.bfloat16),
            pltpu.VMEM((blocks, 8, BLK), jnp.float32),
            pltpu.VMEM((blocks, BLK, HD), jnp.bfloat16),
            pltpu.VMEM((blocks, 8, BLK), jnp.float32),
            dma((6,)),
            dma((chips, 2, 4)),
            dma((chips, 2)),
            dma((chips, 2)),
            dma((chips, 2)),
            dma((2,)),
            dma((blocks, 2)),
            dma((blocks, 2)),
        ],
        compiler_params=pltpu.CompilerParams(collective_id=ident, has_side_effects=True),
    )(queries.reshape(blocks, BLK, HD), keys, values, doc_blocks)


def body(queries, keys, values, doc_blocks):
    starts = doc_blocks.shape[0] - LONGEST + 1
    whole = doc_blocks[:starts] == doc_blocks[LONGEST - 1 :]
    plans = lax.rem(lax.div(lax.iota(jnp.int32, starts), jnp.int32(STARTS)), jnp.int32(len(PLANS)))
    which = jnp.max(jnp.where(whole, plans, 0))
    return lax.switch(
        which, [functools.partial(call, i) for i in range(len(PLANS))], queries, keys, values, doc_blocks
    )


def solution(mesh):
    return jax.shard_map(
        body,
        mesh=mesh,
        in_specs=(P("ctx", "tp"), P("ctx", "tp"), P("ctx", "tp"), P()),
        out_specs=P("ctx", "tp"),
        check_vma=False,
    )
```
